32 devices in a mesh: ctx: 8 (over y, x, core), tp: 4 (over z).
Axes of the slice: x: 2, y: 2, z: 4, core: 2. Of those that a mesh axis runs over, the one named last changes fastest.
Arguments:
- queries: bfloat16 [1024, 32, 128], P('ctx', 'tp'), may hold values from -8 to 8
- window_keys: bfloat16 [1024, 4, 128], P('ctx', 'tp'), may hold values from -8 to 8
- window_values: bfloat16 [1024, 4, 128], P('ctx', 'tp'), may hold values from -6 to 6
- anchor_keys: bfloat16 [512, 4, 128], P('ctx', 'tp'), may hold values from -8 to 8
- anchor_values: bfloat16 [512, 4, 128], P('ctx', 'tp'), may hold values from -6 to 6
- passing_rows: int32 [8, 32], replicated, may hold values from 0 to 127, as said below
- block_of_device: int32 [8], replicated, may hold values from 0 to 7, each once
- out_weight: bfloat16 [4096, 4096], P(None, 'tp'), may hold values from -0.09375 to 0.09375
Outputs:
- mixed: bfloat16 [4096, 1024], P('tp', 'ctx')
The draws below stay inside these ranges and needn't reach their ends.
Inputs may be any that keep to these rules, and one draw needn't show every extreme that they name: `passing_rows`: each row holds 32 different positions. `block_of_device`: every block number appears once.
All inputs are finite; a program needn't handle non-finite values.
Results may differ from the reference program's by a relative error of at most 0.013.
Values may be sent and summed in bfloat16 or wider, within the bound.
No kernel may reach another device: no remote copies, remote signals or barrier semaphores. Data moves between devices by JAX's collectives and lax.ppermute only.
A program may use at most 128 MiB of HBM per device.

```python
import jax
import jax.numpy as jnp
from jax import lax

HD = 128
QH = 32
KVH = 4
DOUT = 4096
TOK_DEV = 128
RETAIN = 32
NBLOCKS = 8
WINDOW = 1024
ANCHOR = 512


def draw_queries(key, part):
    key_main = jax.random.fold_in(key, 17)
    values = jnp.clip(1.6 * jax.random.normal(key_main, (WINDOW, QH, HD)), -8.0, 8.0)
    return values.astype(jnp.bfloat16)


def draw_anchor_keys(key, part):
    key_main = jax.random.fold_in(key, 23)
    values = jnp.clip(1.6 * jax.random.normal(key_main, (ANCHOR, KVH, HD)), -8.0, 8.0)
    return values.astype(jnp.bfloat16)


def draw_passing_rows(key, part):
    row_keys = jax.random.split(jax.random.fold_in(key, 31), NBLOCKS)

    def one_row(row_key):
        return jax.random.permutation(row_key, TOK_DEV)[:RETAIN]
    return jax.vmap(one_row)(row_keys).astype(jnp.int32)


def shard_levels(key, extent, cuts, smallest, top_value):
    gain = 1.0
    for axis_at, parts in cuts:
        draws = jax.random.uniform(jax.random.fold_in(jax.random.fold_in(key, 6), axis_at), (parts,), jnp.float32, smallest / len(cuts), top_value / len(cuts))
        gain = gain * jnp.repeat(jnp.exp(draws), extent[axis_at] // parts).reshape((-1,) + (1,) * (len(extent) - 1 - axis_at))
    return gain


def scatter_about(key, shape, scale, bound, cuts=(), kind=jnp.bfloat16):
    array = scale * jax.random.normal(key, shape, jnp.float32)
    if cuts:
        array = array * shard_levels(key, shape, cuts, -0.22, 0.18)
    return jnp.clip(array, -bound, bound).astype(kind)


def setup_inputs(seed: int = 0) -> dict:
    key_of = jax.random.split(jax.random.key(seed), 9)
    queries = draw_queries(jax.random.fold_in(key_of[8], 71), 0)
    window_keys = scatter_about(key_of[1], (WINDOW, KVH, HD), 1.6, 8.0, ((0, 8), (1, 4)))
    window_values = scatter_about(key_of[2], (WINDOW, KVH, HD), 1.0, 6.0, ((0, 8), (1, 4)))
    anchor_keys = draw_anchor_keys(jax.random.fold_in(key_of[8], 71), 0)
    anchor_values = scatter_about(key_of[4], (ANCHOR, KVH, HD), 1.0, 6.0, ((0, 8), (1, 4)))
    passing_rows = draw_passing_rows(jax.random.fold_in(key_of[8], 71), 0)
    block_of_device = jax.random.permutation(key_of[6], NBLOCKS).astype(jnp.int32)
    out_weight = scatter_about(key_of[7], (DOUT, QH * HD), (QH * HD) ** -0.5, 0.09375, ((1, 4),))
    return {"queries": queries, "window_keys": window_keys, "window_values": window_values, "anchor_keys": anchor_keys, "anchor_values": anchor_values, "passing_rows": passing_rows, "block_of_device": block_of_device, "out_weight": out_weight}


def reference(queries, window_keys, window_values, anchor_keys, anchor_values, passing_rows, block_of_device, out_weight):
    blocks = block_of_device.shape[0]
    tok_rows = queries.shape[0] // blocks
    heads = queries.shape[1]
    kv_heads = window_keys.shape[1]
    head_size = queries.shape[2]
    group_size = heads // kv_heads
    retained = passing_rows.shape[1]
    offsets = jnp.arange(blocks, dtype=jnp.int32)[:, None] * tok_rows
    chosen = (passing_rows + offsets).reshape(-1).astype(jnp.int32)
    pass_keys = jnp.take(window_keys, chosen, axis=0)
    pass_values = jnp.take(window_values, chosen, axis=0)
    pass_blocks = jnp.repeat(block_of_device, retained)
    fixed_keys = jnp.concatenate([anchor_keys, pass_keys], axis=0).astype(jnp.float32)
    fixed_values = jnp.concatenate([anchor_values, pass_values], axis=0).astype(jnp.float32)
    anchor_count = anchor_keys.shape[0]
    fixed_count = fixed_keys.shape[0]
    places = jnp.arange(tok_rows, dtype=jnp.int32)
    causal = places[None, :] <= places[:, None]
    score_scale = head_size ** -0.5

    def one_block(slot_index):
        first_row = slot_index * tok_rows
        query_block = lax.dynamic_slice_in_dim(queries, first_row, tok_rows, 0).astype(jnp.float32)
        query_block = query_block.reshape(tok_rows, kv_heads, group_size, head_size)
        local_keys = lax.dynamic_slice_in_dim(window_keys, first_row, tok_rows, 0).astype(jnp.float32)
        local_values = lax.dynamic_slice_in_dim(window_values, first_row, tok_rows, 0).astype(jnp.float32)
        own_block = block_of_device[slot_index]
        fixed_seen = jnp.concatenate([jnp.ones((anchor_count,), dtype=bool), pass_blocks < own_block])
        visible = jnp.concatenate([jnp.broadcast_to(fixed_seen[None, :], (tok_rows, fixed_count)), causal], axis=1)
        key_rows = jnp.concatenate([fixed_keys, local_keys], axis=0)
        value_rows = jnp.concatenate([fixed_values, local_values], axis=0)
        scores = jnp.einsum('tgjd,ngd->tgjn', query_block, key_rows) * score_scale
        scores = jnp.where(visible[:, None, None, :], scores, -jnp.inf)
        row_max = jnp.max(scores, axis=-1, keepdims=True)
        weights = jnp.exp(scores - row_max)
        total = jnp.sum(weights, axis=-1)
        rounded = lax.optimization_barrier(weights.astype(jnp.bfloat16)).astype(jnp.float32)
        summed = jnp.einsum('tgjn,ngd->tgjd', rounded, value_rows) / total[..., None]
        return summed.reshape(tok_rows, heads * head_size).astype(jnp.bfloat16)

    attended = lax.map(one_block, jnp.arange(blocks, dtype=jnp.int32))
    attended = attended.reshape(blocks * tok_rows, heads * head_size)
    return jnp.dot(out_weight, attended.T, preferred_element_type=jnp.float32).astype(jnp.bfloat16)
```

```python
import functools
import math

import jax
import jax.numpy as jnp
from jax import lax
from jax.experimental import pallas as pl
from jax.experimental.pallas import tpu as pltpu
from jax.sharding import PartitionSpec as P


BF16 = jnp.bfloat16
F32 = jnp.float32
HIDDEN = -1e30
VMEM = pl.BlockSpec(memory_space=pltpu.VMEM)
SMEM = pl.BlockSpec(memory_space=pltpu.SMEM)
ANY = pl.BlockSpec(memory_space=pl.ANY)


def dot(a, b, a_dim, b_dim):
    return lax.dot_general(a, b, (((a_dim,), (b_dim,)), ((), ())), preferred_element_type=F32)


def pack_kernel(rows_ref, wk_ref, wv_ref, ak_ref, av_ref, out_ref):
    anchors, retained = ak_ref.shape[0], rows_ref.shape[1]
    slot = lax.axis_index("ctx")
    chosen = rows_ref[pl.ds(slot, 1), :]
    places = lax.broadcasted_iota(jnp.int32, (wk_ref.shape[0], retained), 0)
    one_hot = (places == chosen).astype(BF16)
    out_ref[0:anchors, :] = ak_ref[...]
    out_ref[anchors : 2 * anchors, :] = av_ref[...]
    first = 2 * anchors
    out_ref[first : first + retained, :] = dot(one_hot, wk_ref[...], 0, 0).astype(BF16)
    out_ref[first + retained :, :] = dot(one_hot, wv_ref[...], 0, 0).astype(BF16)


def project(w_ref, att_ref, out_ref, tile):
    for start in range(0, out_ref.shape[0], tile):
        part = dot(w_ref[start : start + tile, :], att_ref[...], 1, 0)
        out_ref[start : start + tile, :] = part.astype(out_ref.dtype)


def order_of(me):
    far = jnp.where(me % 2 == 0, 3, 0)
    second = jnp.where((me == 0) | (me == 1), 2, 1)
    third = jnp.where(me == 0, 1, jnp.where(me == 1, 3, jnp.where(me == 2, 0, 2)))
    return far, second, third, me


def attend_kernel(
    anchors, blocks_ref, q_ref, g_ref, wk_ref, wv_ref, w_hbm,
    att_ref, first_ref, qf_ref, k_ref, v_ref, w_ref, sem,
):
    slots, packed, size = g_ref.shape
    retained = packed // 2 - anchors
    tok_rows = wk_ref.shape[0]
    heads = q_ref.shape[0] // tok_rows
    chunk_rows = first_ref.shape[0]
    first_chunk = order_of(lax.axis_index("tp"))[0]
    copy = pltpu.make_async_copy(
        w_hbm.at[pl.ds(pl.multiple_of(first_chunk * chunk_rows, 8), chunk_rows), :], w_ref, sem
    )
    copy.start()
    fixed = slots * anchors
    passing = slots * retained
    start = 2 * anchors
    k_ref[0:fixed, :] = g_ref[:, 0:anchors, :].reshape(fixed, size)
    v_ref[0:fixed, :] = g_ref[:, anchors:start, :].reshape(fixed, size)
    k_ref[fixed : fixed + passing, :] = g_ref[:, start : start + retained, :].reshape(passing, size)
    v_ref[fixed : fixed + passing, :] = g_ref[:, start + retained :, :].reshape(passing, size)
    k_ref[fixed + passing :, :] = wk_ref[...]
    v_ref[fixed + passing :, :] = wv_ref[...]
    qf_ref[...] = q_ref[...].astype(F32)
    own_block = blocks_ref[lax.axis_index("ctx")]
    factor = size ** (-0.5) * math.log2(math.e)
    value_cols = v_ref[...].T
    pair = 2
    lanes = pair * tok_rows
    bias = jnp.concatenate(
        [
            jnp.full((retained, lanes), jnp.where(blocks_ref[s] < own_block, 0.0, HIDDEN), F32)
            for s in range(slots)
        ],
        axis=0,
    )
    key_at = lax.broadcasted_iota(jnp.int32, (tok_rows, lanes), 0)
    row_at = lax.broadcasted_iota(jnp.int32, (tok_rows, lanes), 1) % tok_rows
    causal = key_at <= row_at
    for h in range(0, heads, pair):
        q = jnp.concatenate(
            [qf_ref[pl.ds(h + j, tok_rows, stride=heads), :].astype(BF16) for j in range(pair)],
            axis=0,
        )
        seen = dot(k_ref[0:fixed, :], q, 1, 1)
        past = dot(k_ref[fixed : fixed + passing, :], q, 1, 1) + bias
        own = jnp.where(causal, dot(k_ref[fixed + passing :, :], q, 1, 1), HIDDEN)
        scores = jnp.concatenate([seen, past, own], axis=0)
        top = jnp.max(scores, axis=0, keepdims=True)
        weights = jnp.exp2((scores - top) * factor)
        total = jnp.sum(weights, axis=0, keepdims=True)
        summed = dot(value_cols, weights.astype(BF16), 1, 0) / total
        for j in range(pair):
            att_ref[(h + j) * size : (h + j + 1) * size, :] = summed[
                :, j * tok_rows : (j + 1) * tok_rows
            ].astype(BF16)
    copy.wait()
    project(w_ref, att_ref, first_ref, min(256, chunk_rows))


def project_kernel(att_ref, w_hbm, second_ref, third_ref, own_ref, w_ref, sem):
    chunk_rows = own_ref.shape[0]
    chunks = order_of(lax.axis_index("tp"))[1:]
    copies = []
    for slot, chunk in enumerate(chunks):
        begin = pl.multiple_of(chunk * chunk_rows, 8)
        copies.append(
            pltpu.make_async_copy(w_hbm.at[pl.ds(begin, chunk_rows), :], w_ref.at[slot], sem.at[slot])
        )
        copies[-1].start()
    for slot, out_ref in enumerate((second_ref, third_ref, own_ref)):
        copies[slot].wait()
        project(w_ref.at[slot], att_ref, out_ref, min(256, chunk_rows))


def add(*parts):
    return functools.reduce(jnp.add, [p.astype(F32) for p in parts]).astype(BF16)


def body(queries, window_keys, window_values, anchor_keys, anchor_values, passing_rows, block_of_device, out_weight):
    tok_rows, heads, size = queries.shape
    anchors, retained = anchor_keys.shape[0], passing_rows.shape[1]
    slots = block_of_device.shape[0]
    flat = lambda x: x.reshape(x.shape[0], size)
    wk, wv = flat(window_keys), flat(window_values)
    packed = 2 * (anchors + retained)
    block = pl.pallas_call(
        pack_kernel,
        out_shape=jax.ShapeDtypeStruct((packed, size), BF16),
        in_specs=[VMEM] * 5,
        out_specs=VMEM,
        name="pack",
    )(passing_rows, wk, wv, flat(anchor_keys), flat(anchor_values))
    gathered = lax.all_gather(block, "ctx", axis=0, tiled=True).reshape(slots, packed, size)
    tp = lax.axis_size("tp")
    chunk_rows = out_weight.shape[0] // tp
    features = heads * size
    keys = slots * (anchors + retained) + tok_rows
    chunk = jax.ShapeDtypeStruct((chunk_rows, tok_rows), BF16)
    att, first = pl.pallas_call(
        functools.partial(attend_kernel, anchors),
        out_shape=(jax.ShapeDtypeStruct((features, tok_rows), BF16), chunk),
        in_specs=[SMEM, VMEM, VMEM, VMEM, VMEM, ANY],
        out_specs=(VMEM, VMEM),
        scratch_shapes=[
            pltpu.VMEM((tok_rows * heads, size), F32),
            pltpu.VMEM((keys, size), BF16),
            pltpu.VMEM((keys, size), BF16),
            pltpu.VMEM((chunk_rows, features), BF16),
            pltpu.SemaphoreType.DMA,
        ],
        compiler_params=pltpu.CompilerParams(vmem_limit_bytes=50 << 20),
        name="attend",
    )(block_of_device, queries.reshape(tok_rows * heads, size), gathered, wk, wv, out_weight)
    second, third, own = pl.pallas_call(
        project_kernel,
        out_shape=(chunk, chunk, chunk),
        in_specs=[VMEM, ANY],
        out_specs=(VMEM, VMEM, VMEM),
        scratch_shapes=[
            pltpu.VMEM((tp - 1, chunk_rows, features), BF16),
            pltpu.SemaphoreType.DMA((tp - 1,)),
        ],
        compiler_params=pltpu.CompilerParams(vmem_limit_bytes=40 << 20),
        cost_estimate=pl.CostEstimate(
            flops=6 * chunk_rows * features * tok_rows,
            bytes_accessed=6 * chunk_rows * features,
            transcendentals=0,
        ),
        name="project",
    )(att, out_weight)
    send = lambda x, pairs: lax.ppermute(x, "tp", pairs)
    near = send(first, [(0, 1), (1, 0), (2, 3), (3, 2)])
    middle = send(second, [(1, 2), (2, 1)])
    far = send(second, [(0, 2), (3, 1)])
    end = send(third, [(0, 1), (3, 2)])
    relay = send(add(third, near), [(1, 3), (2, 0)])
    me = lax.axis_index("tp")
    at_end = (me == 0) | (me == tp - 1)
    return jnp.where(at_end, add(own, near, relay), add(own, middle, far, end))


def solution(mesh):
    placed = (
        P("ctx", "tp", None),
        P("ctx", "tp", None),
        P("ctx", "tp", None),
        P("ctx", "tp", None),
        P("ctx", "tp", None),
        P(),
        P(),
        P(None, "tp"),
    )
    return jax.shard_map(body, mesh=mesh, in_specs=placed, out_specs=P("tp", "ctx"), check_vma=False)
```

```python
import functools
import math

import jax
import jax.numpy as jnp
from jax import lax
from jax.experimental import pallas as pl
from jax.experimental.pallas import tpu as pltpu
from jax.sharding import PartitionSpec as P


BF16 = jnp.bfloat16
F32 = jnp.float32
HIDDEN = -1e30
VMEM = pl.BlockSpec(memory_space=pltpu.VMEM)
HBM = pl.BlockSpec(memory_space=pltpu.HBM)
DMA = pltpu.SemaphoreType.DMA
PAIR = 2


def dot(a, b, a_dim, b_dim):
    return lax.dot_general(a, b, (((a_dim,), (b_dim,)), ((), ())), preferred_element_type=F32)


def call(kernel, inputs, out_shape, flops, in_specs=None, scratch=()):
    if in_specs:
        inputs = [pltpu.with_memory_space_constraint(x, pltpu.HBM) if s is HBM else x for x, s in zip(inputs, in_specs)]
    moved = sum(x.size * x.dtype.itemsize for x in inputs)
    return pl.pallas_call(
        kernel,
        out_shape=out_shape,
        in_specs=in_specs or [VMEM] * len(inputs),
        out_specs=jax.tree.map(lambda _: VMEM, out_shape),
        scratch_shapes=scratch,
        compiler_params=pltpu.CompilerParams(vmem_limit_bytes=32 << 20),
        cost_estimate=pl.CostEstimate(flops=flops, bytes_accessed=moved, transcendentals=0),
    )(*inputs)


def fetch(pairs, sems):
    copies = [pltpu.make_async_copy(a, b, sems.at[i]) for i, (a, b) in enumerate(pairs)]
    for copy in copies:
        copy.start()
    return copies


def wait(copies):
    for copy in copies:
        copy.wait()


def pack_kernel(rows_hbm, wk_hbm, wv_hbm, ak_hbm, av_hbm, out_ref, rows_ref, wk_ref, wv_ref, sems):
    anchors, retained = ak_hbm.shape[0], rows_ref.shape[1]
    first = 2 * anchors
    pairs = [
        (rows_hbm, rows_ref),
        (wk_hbm, wk_ref),
        (wv_hbm, wv_ref),
        (ak_hbm, out_ref.at[0:anchors, :]),
        (av_hbm, out_ref.at[anchors:first, :]),
    ]
    wait(fetch(pairs, sems))
    slot = lax.axis_index("ctx")
    chosen = rows_ref[pl.ds(slot, 1), :]
    places = lax.broadcasted_iota(jnp.int32, (wk_ref.shape[0], retained), 0)
    one_hot = (places == chosen).astype(BF16)
    out_ref[first : first + retained, :] = dot(one_hot, wk_ref[...], 0, 0).astype(BF16)
    out_ref[first + retained :, :] = dot(one_hot, wv_ref[...], 0, 0).astype(BF16)


def fold(q, before, groups, value_cols, factor):
    scores = jnp.concatenate([mask(dot(keys, q, 1, 1)) for keys, mask in groups], axis=0)
    top = jnp.max(scores, axis=0, keepdims=True)
    if before is not None:
        top = jnp.maximum(top, before[0])
    weights = jnp.exp2((scores - top) * factor)
    total = jnp.sum(weights, axis=0, keepdims=True)
    summed = dot(value_cols, weights.astype(BF16), 1, 0)
    if before is not None:
        fade = jnp.exp2((before[0] - top) * factor)
        total = total + before[1] * fade
        summed = summed + before[2] * fade
    return top, total, summed


def factor_of(size):
    return size ** (-0.5) * math.log2(math.e)


def chunk_of(w_hbm, at, rows):
    chunk = order_of(lax.axis_index("tp"))[at]
    return w_hbm.at[pl.ds(pl.multiple_of(chunk * rows, 16), rows), :]


def own_kernel(blocks_hbm, q_hbm, wk_hbm, wv_hbm, w_hbm, qh_ref, hide_ref, w_ref, top_ref, total_ref, summed_ref,
               blocks_ref, q_ref, wk_ref, wv_ref, qf_ref, sems):
    pairs = [(blocks_hbm, blocks_ref), (q_hbm, q_ref), (wk_hbm, wk_ref), (wv_hbm, wv_ref)]
    pairs.append((chunk_of(w_hbm, 0, w_ref.shape[0]), w_ref))
    copies = fetch(pairs, sems)
    wait(copies[:-1])
    tok_rows, size = wk_ref.shape
    heads = q_ref.shape[0] // tok_rows
    slot = lax.axis_index("ctx")
    own_block = blocks_ref[slot]
    for j in range(blocks_ref.shape[0]):
        bias = jnp.where(blocks_ref[slot ^ j] < own_block, 0.0, HIDDEN)
        hide_ref[j : j + 1, :] = jnp.full((1, hide_ref.shape[1]), bias, F32)
    qf_ref[...] = q_ref[...].astype(F32)
    lanes = PAIR * tok_rows
    key_at = lax.broadcasted_iota(jnp.int32, (tok_rows, lanes), 0)
    row_at = lax.broadcasted_iota(jnp.int32, (tok_rows, lanes), 1) % tok_rows
    causal = key_at <= row_at
    value_cols = wv_ref[...].T
    for h in range(0, heads, PAIR):
        for j in range(h, h + PAIR):
            qh_ref[j * tok_rows : (j + 1) * tok_rows, :] = qf_ref[
                pl.ds(j, tok_rows, stride=heads), :
            ].astype(BF16)
        cols = slice(h * tok_rows, (h + PAIR) * tok_rows)
        groups = [(wk_ref[...], lambda s: jnp.where(causal, s, HIDDEN))]
        state = fold(qh_ref[cols, :], None, groups, value_cols, factor_of(size))
        top_ref[:, cols], total_ref[:, cols], summed_ref[:, cols] = state
    wait(copies[-1:])


def rows_of(block_ref, anchors, retained):
    slots, _, size = block_ref.shape
    first = 2 * anchors
    take = lambda a, n: block_ref[:, a : a + n, :].reshape(slots * n, size)
    seen, past = take(0, anchors), take(first, retained)
    values = jnp.concatenate([take(anchors, anchors), take(first + retained, retained)], axis=0)
    return seen, past, values.T


def hidden_rows(hide_ref, order, retained, lanes):
    width = hide_ref.shape[1]
    rows = [jnp.broadcast_to(hide_ref[j : j + 1, :], (retained, width)) for j in order]
    column = jnp.concatenate(rows, axis=0)
    return jnp.concatenate([column] * (lanes // width), axis=1)


def fold_blocks(order, anchors, retained, qh_ref, hide_ref, block_ref, state_refs, finish):
    top_ref, total_ref, summed_ref = state_refs
    tok_rows = hide_ref.shape[1]
    size = qh_ref.shape[1]
    heads = qh_ref.shape[0] // tok_rows
    seen, past, value_cols = rows_of(block_ref, anchors, retained)
    bias = hidden_rows(hide_ref, order, retained, PAIR * tok_rows)
    groups = [(seen, lambda s: s), (past, lambda s: s + bias)]
    for h in range(0, heads, PAIR):
        cols = slice(h * tok_rows, (h + PAIR) * tok_rows)
        before = (top_ref[:, cols], total_ref[:, cols], summed_ref[:, cols])
        finish(h, cols, fold(qh_ref[cols, :], before, groups, value_cols, factor_of(size)))


def early_kernel(order, anchors, retained, qh_ref, hide_ref, block_ref, top0, total0, summed0, w_hbm,
                 w_ref, top_ref, total_ref, summed_ref, sems):
    copies = fetch([(chunk_of(w_hbm, 1, w_ref.shape[0]), w_ref)], sems)

    def finish(h, cols, state):
        top_ref[:, cols], total_ref[:, cols], summed_ref[:, cols] = state

    fold_blocks(order, anchors, retained, qh_ref, hide_ref, block_ref, (top0, total0, summed0), finish)
    wait(copies)


def project(w_ref, att_ref, out_ref):
    rows = out_ref.shape[0]
    tile = min(256, rows)
    for start in range(0, rows, tile):
        part = dot(w_ref[start : start + tile, :], att_ref[...], 1, 0)
        out_ref[start : start + tile, :] = part.astype(out_ref.dtype)


def order_of(me):
    far = jnp.where(me % 2 == 0, 3, 0)
    second = jnp.where((me == 0) | (me == 1), 2, 1)
    third = jnp.where(me == 0, 1, jnp.where(me == 1, 3, jnp.where(me == 2, 0, 2)))
    return far, second, third, me


def late_kernel(order, anchors, retained, qh_ref, hide_ref, block_ref, top0, total0, summed0, w_ref, w_hbm,
                att_ref, first_ref, next_ref, sems):
    copies = fetch([(chunk_of(w_hbm, 2, next_ref.shape[0]), next_ref)], sems)
    tok_rows = hide_ref.shape[1]
    size = qh_ref.shape[1]

    def finish(h, cols, state):
        _, total, summed = state
        attended = (summed / total).astype(BF16)
        for j in range(PAIR):
            att_ref[(h + j) * size : (h + j + 1) * size, :] = attended[:, j * tok_rows : (j + 1) * tok_rows]

    fold_blocks(order, anchors, retained, qh_ref, hide_ref, block_ref, (top0, total0, summed0), finish)
    project(w_ref, att_ref, first_ref)
    wait(copies)


def second_kernel(att_ref, w_ref, w_hbm, out_ref, next_ref, sems):
    copies = fetch([(chunk_of(w_hbm, 3, next_ref.shape[0]), next_ref)], sems)
    project(w_ref, att_ref, out_ref)
    wait(copies)


def third_kernel(att_ref, w_ref, last_ref, out_ref, own_ref):
    project(w_ref, att_ref, out_ref)
    project(last_ref, att_ref, own_ref)


def add(*parts):
    return functools.reduce(jnp.add, [p.astype(F32) for p in parts]).astype(BF16)


def layer(queries, window_keys, window_values, anchor_keys, anchor_values, passing_rows, block_of_device, out_weight):
    tok_rows, heads, size = queries.shape
    anchors, retained = anchor_keys.shape[0], passing_rows.shape[1]
    slots = block_of_device.shape[0]
    flat = lambda x: x.reshape(x.shape[0], size)
    wk, wv = flat(window_keys), flat(window_values)
    packed = 2 * (anchors + retained)
    shape = jax.ShapeDtypeStruct
    tp = lax.axis_size("tp")
    chunk_rows = out_weight.shape[0] // tp
    features = heads * size
    row = lambda n: shape((n, size), BF16)
    chunk, weight = shape((chunk_rows, tok_rows), BF16), shape((chunk_rows, features), BF16)
    chunk_flops = 2 * chunk_rows * tok_rows * features
    block = call(
        pack_kernel,
        (passing_rows, wk, wv, flat(anchor_keys), flat(anchor_values)),
        row(packed),
        4 * retained * tok_rows * size,
        in_specs=[HBM] * 5,
        scratch=[
            pltpu.VMEM(passing_rows.shape, jnp.int32),
            pltpu.VMEM((tok_rows, size), BF16),
            pltpu.VMEM((tok_rows, size), BF16),
            DMA((5,)),
        ],
    )
    query_rows = heads * tok_rows
    stats = (
        shape((1, query_rows), F32),
        shape((1, query_rows), F32),
        shape((size, query_rows), F32),
    )
    qh, hide, w_first, *state = call(
        own_kernel,
        (block_of_device, queries.reshape(query_rows, size), wk, wv, out_weight),
        (row(query_rows), shape((slots, tok_rows), F32), weight, *stats),
        4 * query_rows * tok_rows * size,
        in_specs=[HBM] * 5,
        scratch=[
            pltpu.SMEM((slots,), jnp.int32),
            pltpu.VMEM((query_rows, size), BF16),
            pltpu.VMEM((tok_rows, size), BF16),
            pltpu.VMEM((tok_rows, size), BF16),
            pltpu.VMEM((query_rows, size), F32),
            DMA((5,)),
        ],
    )
    order = [0]
    step = slots // 2
    held = block
    while step > 1:
        other = lax.ppermute(held, "ctx", [(i, i ^ step) for i in range(slots)])
        held = jnp.concatenate([held, other], axis=0)
        order = order + [j ^ step for j in order]
        step //= 2
    other = lax.ppermute(held, "ctx", [(i, i ^ step) for i in range(slots)])
    late_order = [j ^ step for j in order]
    half = (slots // 2, packed, size)
    fold_flops = 4 * query_rows * (slots // 2) * (anchors + retained) * size
    w_second, *state = call(
        functools.partial(early_kernel, order, anchors, retained),
        (qh, hide, held.reshape(half), *state, out_weight),
        (weight, *stats),
        fold_flops,
        in_specs=[VMEM] * 6 + [HBM],
        scratch=[DMA((1,))],
    )
    att, first, w_third = call(
        functools.partial(late_kernel, late_order, anchors, retained),
        (qh, hide, other.reshape(half), *state, w_first, out_weight),
        (shape((features, tok_rows), BF16), chunk, weight),
        fold_flops + chunk_flops,
        in_specs=[VMEM] * 7 + [HBM],
        scratch=[DMA((1,))],
    )
    send = lambda x, pairs: lax.ppermute(x, "tp", pairs)
    near = send(first, [(0, 1), (1, 0), (2, 3), (3, 2)])
    second, w_own = call(
        second_kernel,
        (att, w_second, out_weight),
        (chunk, weight),
        chunk_flops,
        in_specs=[VMEM, VMEM, HBM],
        scratch=[DMA((1,))],
    )
    middle = send(second, [(1, 2), (2, 1)])
    far = send(second, [(0, 2), (3, 1)])
    third, own = call(third_kernel, (att, w_third, w_own), (chunk, chunk), 2 * chunk_flops)
    end = send(third, [(0, 1), (3, 2)])
    relay = send(add(third, near), [(1, 3), (2, 0)])
    me = lax.axis_index("tp")
    at_end = (me == 0) | (me == tp - 1)
    return jnp.where(at_end, add(own, near, relay), add(own, middle, far, end))


def solution(mesh):
    placed = (
        P("ctx", "tp", None),
        P("ctx", "tp", None),
        P("ctx", "tp", None),
        P("ctx", "tp", None),
        P("ctx", "tp", None),
        P(),
        P(),
        P(None, "tp"),
    )
    return jax.shard_map(layer, mesh=mesh, in_specs=placed, out_specs=P("tp", "ctx"), check_vma=False)
```

```python
import functools
import math

import jax
import jax.numpy as jnp
from jax import lax
from jax.experimental import pallas as pl
from jax.experimental.pallas import tpu as pltpu
from jax.sharding import PartitionSpec as P


BF16 = jnp.bfloat16
F32 = jnp.float32
HIDDEN = -1e30
VMEM = pl.BlockSpec(memory_space=pltpu.VMEM)
HBM = pl.BlockSpec(memory_space=pltpu.HBM)
DMA = pltpu.SemaphoreType.DMA
PAIR = 2
PARTS = 4


def dot(a, b, a_dim, b_dim):
    return lax.dot_general(a, b, (((a_dim,), (b_dim,)), ((), ())), preferred_element_type=F32)


def call(kernel, inputs, out_shape, flops, in_specs=None, scratch=()):
    if in_specs:
        inputs = [pltpu.with_memory_space_constraint(x, pltpu.HBM) if s is HBM else x for x, s in zip(inputs, in_specs)]
    moved = sum(x.size * x.dtype.itemsize for x in inputs)
    return pl.pallas_call(
        kernel,
        out_shape=out_shape,
        in_specs=in_specs or [VMEM] * len(inputs),
        out_specs=jax.tree.map(lambda _: VMEM, out_shape),
        scratch_shapes=scratch,
        compiler_params=pltpu.CompilerParams(vmem_limit_bytes=32 << 20),
        cost_estimate=pl.CostEstimate(flops=flops, bytes_accessed=moved, transcendentals=0),
    )(*inputs)


def fetch(pairs, sems):
    copies = [pltpu.make_async_copy(a, b, sems.at[i]) for i, (a, b) in enumerate(pairs)]
    for copy in copies:
        copy.start()
    return copies


def wait(copies):
    for copy in copies:
        copy.wait()


def pack_kernel(rows_hbm, wk_hbm, wv_hbm, ak_hbm, av_hbm, out_ref, rows_ref, wk_ref, wv_ref, sems):
    anchors, retained = ak_hbm.shape[0], rows_ref.shape[1]
    first = 2 * anchors
    pairs = [
        (rows_hbm, rows_ref),
        (wk_hbm, wk_ref),
        (wv_hbm, wv_ref),
        (ak_hbm, out_ref.at[0:anchors, :]),
        (av_hbm, out_ref.at[anchors:first, :]),
    ]
    wait(fetch(pairs, sems))
    slot = lax.axis_index("ctx")
    chosen = rows_ref[pl.ds(slot, 1), :]
    places = lax.broadcasted_iota(jnp.int32, (wk_ref.shape[0], retained), 0)
    one_hot = (places == chosen).astype(BF16)
    out_ref[first : first + retained, :] = dot(one_hot, wk_ref[...], 0, 0).astype(BF16)
    out_ref[first + retained :, :] = dot(one_hot, wv_ref[...], 0, 0).astype(BF16)


def fold(q, before, groups, value_cols, factor):
    scores = jnp.concatenate([mask(dot(keys, q, 1, 1)) for keys, mask in groups], axis=0)
    top = jnp.max(scores, axis=0, keepdims=True)
    if before is not None:
        top = jnp.maximum(top, before[0])
    weights = jnp.exp2((scores - top) * factor)
    total = jnp.sum(weights, axis=0, keepdims=True)
    summed = dot(value_cols, weights.astype(BF16), 1, 0)
    if before is not None:
        fade = jnp.exp2((before[0] - top) * factor)
        total = total + before[1] * fade
        summed = summed + before[2] * fade
    return top, total, summed


def factor_of(size):
    return size ** (-0.5) * math.log2(math.e)


def parts_of(w_hbm, at, w_ref):
    rows = w_ref.shape[0]
    chunk = order_of(lax.axis_index("tp"))[at]
    part = rows // PARTS
    return [
        (w_hbm.at[pl.ds(pl.multiple_of(chunk * rows + i * part, 16), part), :], w_ref.at[i * part : (i + 1) * part, :])
        for i in range(PARTS)
    ]


def own_kernel(blocks_hbm, q_hbm, wk_hbm, wv_hbm, w_hbm, qh_ref, hide_ref, w_ref, top_ref, total_ref, summed_ref,
               blocks_ref, q_ref, wk_ref, wv_ref, qf_ref, sems):
    pairs = [(blocks_hbm, blocks_ref), (q_hbm, q_ref), (wk_hbm, wk_ref), (wv_hbm, wv_ref)]
    copies = fetch(pairs + parts_of(w_hbm, 0, w_ref), sems)
    wait(copies[: len(pairs)])
    tok_rows, size = wk_ref.shape
    heads = q_ref.shape[0] // tok_rows
    slot = lax.axis_index("ctx")
    own_block = blocks_ref[slot]
    for j in range(blocks_ref.shape[0]):
        bias = jnp.where(blocks_ref[slot ^ j] < own_block, 0.0, HIDDEN)
        hide_ref[j : j + 1, :] = jnp.full((1, hide_ref.shape[1]), bias, F32)
    qf_ref[...] = q_ref[...].astype(F32)
    lanes = PAIR * tok_rows
    key_at = lax.broadcasted_iota(jnp.int32, (tok_rows, lanes), 0)
    row_at = lax.broadcasted_iota(jnp.int32, (tok_rows, lanes), 1) % tok_rows
    causal = key_at <= row_at
    value_cols = wv_ref[...].T
    for h in range(0, heads, PAIR):
        for j in range(h, h + PAIR):
            qh_ref[j * tok_rows : (j + 1) * tok_rows, :] = qf_ref[
                pl.ds(j, tok_rows, stride=heads), :
            ].astype(BF16)
        cols = slice(h * tok_rows, (h + PAIR) * tok_rows)
        groups = [(wk_ref[...], lambda s: jnp.where(causal, s, HIDDEN))]
        state = fold(qh_ref[cols, :], None, groups, value_cols, factor_of(size))
        top_ref[:, cols], total_ref[:, cols], summed_ref[:, cols] = state
    wait(copies[len(pairs) :])


def rows_of(block_ref, anchors, retained):
    slots, _, size = block_ref.shape
    first = 2 * anchors
    take = lambda a, n: block_ref[:, a : a + n, :].reshape(slots * n, size)
    seen, past = take(0, anchors), take(first, retained)
    values = jnp.concatenate([take(anchors, anchors), take(first + retained, retained)], axis=0)
    return seen, past, values.T


def hidden_rows(hide_ref, order, retained, lanes):
    width = hide_ref.shape[1]
    rows = [jnp.broadcast_to(hide_ref[j : j + 1, :], (retained, width)) for j in order]
    column = jnp.concatenate(rows, axis=0)
    return jnp.concatenate([column] * (lanes // width), axis=1)


def fold_blocks(order, anchors, retained, qh_ref, hide_ref, block_ref, state_refs, finish):
    top_ref, total_ref, summed_ref = state_refs
    tok_rows = hide_ref.shape[1]
    size = qh_ref.shape[1]
    heads = qh_ref.shape[0] // tok_rows
    seen, past, value_cols = rows_of(block_ref, anchors, retained)
    bias = hidden_rows(hide_ref, order, retained, PAIR * tok_rows)
    groups = [(seen, lambda s: s), (past, lambda s: s + bias)]
    for h in range(0, heads, PAIR):
        cols = slice(h * tok_rows, (h + PAIR) * tok_rows)
        before = (top_ref[:, cols], total_ref[:, cols], summed_ref[:, cols])
        finish(h, cols, fold(qh_ref[cols, :], before, groups, value_cols, factor_of(size)))


def early_kernel(order, anchors, retained, qh_ref, hide_ref, block_ref, top0, total0, summed0,
                 top_ref, total_ref, summed_ref):
    def finish(h, cols, state):
        top_ref[:, cols], total_ref[:, cols], summed_ref[:, cols] = state

    fold_blocks(order, anchors, retained, qh_ref, hide_ref, block_ref, (top0, total0, summed0), finish)


def fetch_kernel(held_ref, w_hbm, second_ref, third_ref, sems):
    wait(fetch(parts_of(w_hbm, 1, second_ref) + parts_of(w_hbm, 2, third_ref), sems))


def project(w_ref, att_ref, out_ref):
    rows = out_ref.shape[0]
    tile = min(256, rows)
    for start in range(0, rows, tile):
        part = dot(w_ref[start : start + tile, :], att_ref[...], 1, 0)
        out_ref[start : start + tile, :] = part.astype(out_ref.dtype)


def order_of(me):
    far = jnp.where(me % 2 == 0, 3, 0)
    second = jnp.where((me == 0) | (me == 1), 2, 1)
    third = jnp.where(me == 0, 1, jnp.where(me == 1, 3, jnp.where(me == 2, 0, 2)))
    return far, second, third, me


def late_kernel(order, anchors, retained, qh_ref, hide_ref, block_ref, top0, total0, summed0, w_ref,
                att_ref, first_ref):
    tok_rows = hide_ref.shape[1]
    size = qh_ref.shape[1]

    def finish(h, cols, state):
        _, total, summed = state
        attended = (summed / total).astype(BF16)
        for j in range(PAIR):
            att_ref[(h + j) * size : (h + j + 1) * size, :] = attended[:, j * tok_rows : (j + 1) * tok_rows]

    fold_blocks(order, anchors, retained, qh_ref, hide_ref, block_ref, (top0, total0, summed0), finish)
    project(w_ref, att_ref, first_ref)


def second_kernel(att_ref, w_ref, out_ref):
    project(w_ref, att_ref, out_ref)


def third_kernel(att_ref, w_ref, w_hbm, out_ref, own_ref, last_ref, sems):
    copies = fetch(parts_of(w_hbm, 3, last_ref), sems)
    project(w_ref, att_ref, out_ref)
    wait(copies)
    project(last_ref, att_ref, own_ref)


def add(*parts):
    return functools.reduce(jnp.add, [p.astype(F32) for p in parts]).astype(BF16)


def layer(queries, window_keys, window_values, anchor_keys, anchor_values, passing_rows, block_of_device, out_weight):
    tok_rows, heads, size = queries.shape
    anchors, retained = anchor_keys.shape[0], passing_rows.shape[1]
    slots = block_of_device.shape[0]
    flat = lambda x: x.reshape(x.shape[0], size)
    wk, wv = flat(window_keys), flat(window_values)
    packed = 2 * (anchors + retained)
    shape = jax.ShapeDtypeStruct
    tp = lax.axis_size("tp")
    chunk_rows = out_weight.shape[0] // tp
    features = heads * size
    row = lambda n: shape((n, size), BF16)
    chunk, weight = shape((chunk_rows, tok_rows), BF16), shape((chunk_rows, features), BF16)
    chunk_flops = 2 * chunk_rows * tok_rows * features
    block = call(
        pack_kernel,
        (passing_rows, wk, wv, flat(anchor_keys), flat(anchor_values)),
        row(packed),
        4 * retained * tok_rows * size,
        in_specs=[HBM] * 5,
        scratch=[
            pltpu.VMEM(passing_rows.shape, jnp.int32),
            pltpu.VMEM((tok_rows, size), BF16),
            pltpu.VMEM((tok_rows, size), BF16),
            DMA((5,)),
        ],
    )
    query_rows = heads * tok_rows
    stats = (
        shape((1, query_rows), F32),
        shape((1, query_rows), F32),
        shape((size, query_rows), F32),
    )
    qh, hide, w_first, *state = call(
        own_kernel,
        (block_of_device, queries.reshape(query_rows, size), wk, wv, out_weight),
        (row(query_rows), shape((slots, tok_rows), F32), weight, *stats),
        4 * query_rows * tok_rows * size,
        in_specs=[HBM] * 5,
        scratch=[
            pltpu.SMEM((slots,), jnp.int32),
            pltpu.VMEM((query_rows, size), BF16),
            pltpu.VMEM((tok_rows, size), BF16),
            pltpu.VMEM((tok_rows, size), BF16),
            pltpu.VMEM((query_rows, size), F32),
            DMA((4 + PARTS,)),
        ],
    )
    order = [0]
    step = slots // 2
    held = block
    while step > 1:
        other = lax.ppermute(held, "ctx", [(i, i ^ step) for i in range(slots)])
        held = jnp.concatenate([held, other], axis=0)
        order = order + [j ^ step for j in order]
        step //= 2
    w_second, w_third = call(
        fetch_kernel, (hide, out_weight), (weight, weight), 0, in_specs=[VMEM, HBM], scratch=[DMA((2 * PARTS,))]
    )
    other = lax.ppermute(held, "ctx", [(i, i ^ step) for i in range(slots)])
    late_order = [j ^ step for j in order]
    half = (slots // 2, packed, size)
    fold_flops = 4 * query_rows * (slots // 2) * (anchors + retained) * size
    state = call(
        functools.partial(early_kernel, order, anchors, retained),
        (qh, hide, held.reshape(half), *state),
        stats,
        fold_flops,
    )
    att, first = call(
        functools.partial(late_kernel, late_order, anchors, retained),
        (qh, hide, other.reshape(half), *state, w_first),
        (shape((features, tok_rows), BF16), chunk),
        fold_flops + chunk_flops,
    )
    send = lambda x, pairs: lax.ppermute(x, "tp", pairs)
    near = send(first, [(0, 1), (1, 0), (2, 3), (3, 2)])
    second = call(second_kernel, (att, w_second), chunk, chunk_flops)
    middle = send(second, [(1, 2), (2, 1)])
    far = send(second, [(0, 2), (3, 1)])
    third, own = call(
        third_kernel,
        (att, w_third, out_weight),
        (chunk, chunk),
        2 * chunk_flops,
        in_specs=[VMEM, VMEM, HBM],
        scratch=[pltpu.VMEM((chunk_rows, features), BF16), DMA((PARTS,))],
    )
    end = send(third, [(0, 1), (3, 2)])
    relay = send(add(third, near), [(1, 3), (2, 0)])
    me = lax.axis_index("tp")
    at_end = (me == 0) | (me == tp - 1)
    return jnp.where(at_end, add(own, near, relay), add(own, middle, far, end))


def solution(mesh):
    placed = (
        P("ctx", "tp", None),
        P("ctx", "tp", None),
        P("ctx", "tp", None),
        P("ctx", "tp", None),
        P("ctx", "tp", None),
        P(),
        P(),
        P(None, "tp"),
    )
    return jax.shard_map(layer, mesh=mesh, in_specs=placed, out_specs=P("tp", "ctx"), check_vma=False)
```

```python
import functools
import math

import jax
import jax.numpy as jnp
from jax import lax
from jax.experimental import pallas as pl
from jax.experimental.pallas import tpu as pltpu
from jax.sharding import PartitionSpec as P


BF16 = jnp.bfloat16
F32 = jnp.float32
HIDDEN = -1e30
VMEM = pl.BlockSpec(memory_space=pltpu.VMEM)
HBM = pl.BlockSpec(memory_space=pltpu.HBM)
DMA = pltpu.SemaphoreType.DMA
PAIR = 2
PARTS = 4
RELAY_PARTS, ALL_PARTS = 5, 8


def dot(a, b, a_dim, b_dim):
    return lax.dot_general(a, b, (((a_dim,), (b_dim,)), ((), ())), preferred_element_type=F32)


def call(kernel, inputs, out_shape, flops, in_specs=None, scratch=()):
    if in_specs:
        inputs = [pltpu.with_memory_space_constraint(x, pltpu.HBM) if s is HBM else x for x, s in zip(inputs, in_specs)]
    moved = sum(x.size * x.dtype.itemsize for x in inputs)
    return pl.pallas_call(
        kernel,
        out_shape=out_shape,
        in_specs=in_specs or [VMEM] * len(inputs),
        out_specs=jax.tree.map(lambda _: VMEM, out_shape),
        scratch_shapes=scratch,
        compiler_params=pltpu.CompilerParams(vmem_limit_bytes=32 << 20),
        cost_estimate=pl.CostEstimate(flops=flops, bytes_accessed=moved, transcendentals=0),
    )(*inputs)


def fetch(pairs, sems):
    copies = [pltpu.make_async_copy(a, b, sems.at[i]) for i, (a, b) in enumerate(pairs)]
    for copy in copies:
        copy.start()
    return copies


def wait(copies):
    for copy in copies:
        copy.wait()


def pack_kernel(rows_hbm, wk_hbm, wv_hbm, ak_hbm, av_hbm, out_ref, rows_ref, wk_ref, wv_ref, sems):
    anchors, retained = ak_hbm.shape[0], rows_ref.shape[1]
    first = 2 * anchors
    pairs = [
        (rows_hbm, rows_ref),
        (wk_hbm, wk_ref),
        (wv_hbm, wv_ref),
        (ak_hbm, out_ref.at[0:anchors, :]),
        (av_hbm, out_ref.at[anchors:first, :]),
    ]
    wait(fetch(pairs, sems))
    slot = lax.axis_index("ctx")
    chosen = rows_ref[pl.ds(slot, 1), :]
    places = lax.broadcasted_iota(jnp.int32, (wk_ref.shape[0], retained), 0)
    one_hot = (places == chosen).astype(BF16)
    out_ref[first : first + retained, :] = dot(one_hot, wk_ref[...], 0, 0).astype(BF16)
    out_ref[first + retained :, :] = dot(one_hot, wv_ref[...], 0, 0).astype(BF16)


def fold(q, before, groups, value_cols, factor):
    scores = jnp.concatenate([mask(dot(keys, q, 1, 1)) for keys, mask in groups], axis=0)
    top = jnp.max(scores, axis=0, keepdims=True)
    if before is not None:
        top = jnp.maximum(top, before[0])
    weights = jnp.exp2((scores - top) * factor)
    total = jnp.sum(weights, axis=0, keepdims=True)
    summed = dot(value_cols, weights.astype(BF16), 1, 0)
    if before is not None:
        fade = jnp.exp2((before[0] - top) * factor)
        total = total + before[1] * fade
        summed = summed + before[2] * fade
    return top, total, summed


def factor_of(size):
    return size ** (-0.5) * math.log2(math.e)


def parts_of(w_hbm, mask, w_ref):
    rows = w_ref.shape[0]
    begin = (lax.axis_index("tp") ^ mask) * rows
    part = rows // PARTS
    return [
        (w_hbm.at[pl.ds(pl.multiple_of(begin + i, 16), part), :], w_ref.at[i : i + part, :])
        for i in range(0, rows, part)
    ]


def own_kernel(blocks_hbm, q_hbm, wk_hbm, wv_hbm, w_hbm, qh_ref, hide_ref, w_ref, top_ref, total_ref, summed_ref,
               blocks_ref, q_ref, wk_ref, wv_ref, qf_ref, sems):
    pairs = [(blocks_hbm, blocks_ref), (q_hbm, q_ref), (wk_hbm, wk_ref), (wv_hbm, wv_ref)]
    copies = fetch(pairs + parts_of(w_hbm, 3, w_ref), sems)
    wait(copies[: len(pairs)])
    tok_rows, size = wk_ref.shape
    heads = q_ref.shape[0] // tok_rows
    slot = lax.axis_index("ctx")
    own_block = blocks_ref[slot]
    for j in range(blocks_ref.shape[0]):
        bias = jnp.where(blocks_ref[slot ^ j] < own_block, 0.0, HIDDEN)
        hide_ref[j : j + 1, :] = jnp.full((1, hide_ref.shape[1]), bias, F32)
    qf_ref[...] = q_ref[...].astype(F32)
    lanes = PAIR * tok_rows
    key_at = lax.broadcasted_iota(jnp.int32, (tok_rows, lanes), 0)
    row_at = lax.broadcasted_iota(jnp.int32, (tok_rows, lanes), 1) % tok_rows
    causal = key_at <= row_at
    value_cols = wv_ref[...].T
    for h in range(0, heads, PAIR):
        for j in range(h, h + PAIR):
            qh_ref[j * tok_rows : (j + 1) * tok_rows, :] = qf_ref[
                pl.ds(j, tok_rows, stride=heads), :
            ].astype(BF16)
        cols = slice(h * tok_rows, (h + PAIR) * tok_rows)
        groups = [(wk_ref[...], lambda s: jnp.where(causal, s, HIDDEN))]
        state = fold(qh_ref[cols, :], None, groups, value_cols, factor_of(size))
        top_ref[:, cols], total_ref[:, cols], summed_ref[:, cols] = state
    wait(copies[len(pairs) :])


def rows_of(block_ref, anchors, retained):
    slots, _, size = block_ref.shape
    first = 2 * anchors
    take = lambda a, n: block_ref[:, a : a + n, :].reshape(slots * n, size)
    seen, past = take(0, anchors), take(first, retained)
    values = jnp.concatenate([take(anchors, anchors), take(first + retained, retained)], axis=0)
    return seen, past, values.T


def hidden_rows(hide_ref, order, retained, lanes):
    width = hide_ref.shape[1]
    rows = [jnp.broadcast_to(hide_ref[j : j + 1, :], (retained, width)) for j in order]
    column = jnp.concatenate(rows, axis=0)
    return jnp.concatenate([column] * (lanes // width), axis=1)


def fold_blocks(order, anchors, retained, qh_ref, hide_ref, block_ref, state_refs, finish):
    top_ref, total_ref, summed_ref = state_refs
    tok_rows = hide_ref.shape[1]
    size = qh_ref.shape[1]
    heads = qh_ref.shape[0] // tok_rows
    seen, past, value_cols = rows_of(block_ref, anchors, retained)
    bias = hidden_rows(hide_ref, order, retained, PAIR * tok_rows)
    groups = [(seen, lambda s: s), (past, lambda s: s + bias)]
    for h in range(0, heads, PAIR):
        cols = slice(h * tok_rows, (h + PAIR) * tok_rows)
        before = (top_ref[:, cols], total_ref[:, cols], summed_ref[:, cols])
        finish(h, cols, fold(qh_ref[cols, :], before, groups, value_cols, factor_of(size)))


def early_kernel(order, anchors, retained, qh_ref, hide_ref, block_ref, top0, total0, summed0,
                 top_ref, total_ref, summed_ref):
    def finish(h, cols, state):
        top_ref[:, cols], total_ref[:, cols], summed_ref[:, cols] = state

    fold_blocks(order, anchors, retained, qh_ref, hide_ref, block_ref, (top0, total0, summed0), finish)


def fetch_kernel(hide_ref, w_hbm, far_ref, near_ref, sems):
    wait(fetch(parts_of(w_hbm, 2, far_ref) + parts_of(w_hbm, 1, near_ref), sems))


def project(w_ref, first, att_ref, out_ref):
    rows = out_ref.shape[0]
    tile = math.gcd(256, rows)
    for start in range(0, rows, tile):
        part = dot(w_ref[first + start : first + start + tile, :], att_ref[...], 1, 0)
        out_ref[start : start + tile, :] = part.astype(out_ref.dtype)


def late_kernel(order, anchors, retained, qh_ref, hide_ref, block_ref, top0, total0, summed0, w_ref,
                att_ref, first_ref):
    tok_rows = hide_ref.shape[1]
    size = qh_ref.shape[1]

    def finish(h, cols, state):
        _, total, summed = state
        attended = (summed / total).astype(BF16)
        for j in range(PAIR):
            att_ref[(h + j) * size : (h + j + 1) * size, :] = attended[:, j * tok_rows : (j + 1) * tok_rows]

    fold_blocks(order, anchors, retained, qh_ref, hide_ref, block_ref, (top0, total0, summed0), finish)
    project(w_ref, 0, att_ref, first_ref)


def direct_kernel(att_ref, farther_w, far_w, farther_ref, far_ref):
    for w_ref, out_ref in ((farther_w, farther_ref), (far_w, far_ref)):
        project(w_ref, w_ref.shape[0] - out_ref.shape[0], att_ref, out_ref)


def later_kernel(att_ref, far_w, near_w, across_ref, near_ref):
    project(far_w, 0, att_ref, across_ref)
    project(near_w, 0, att_ref, near_ref)


def own_chunk_kernel(att_ref, w_hbm, out_ref, w_ref, sems):
    wait(fetch(parts_of(w_hbm, 0, w_ref), sems))
    project(w_ref, 0, att_ref, out_ref)


def add(*parts):
    return functools.reduce(jnp.add, [p.astype(F32) for p in parts]).astype(BF16)


def layer(queries, window_keys, window_values, anchor_keys, anchor_values, passing_rows, block_of_device, out_weight):
    tok_rows, heads, size = queries.shape
    anchors, retained = anchor_keys.shape[0], passing_rows.shape[1]
    slots = block_of_device.shape[0]
    flat = lambda x: x.reshape(x.shape[0], size)
    wk, wv = flat(window_keys), flat(window_values)
    packed = 2 * (anchors + retained)
    shape = jax.ShapeDtypeStruct
    tp = lax.axis_size("tp")
    chunk_rows = out_weight.shape[0] // tp
    features = heads * size
    row = lambda n: shape((n, size), BF16)
    chunk, weight = shape((chunk_rows, tok_rows), BF16), shape((chunk_rows, features), BF16)
    relay_rows = chunk_rows * RELAY_PARTS // ALL_PARTS
    relayed = shape((relay_rows, tok_rows), BF16)
    direct = shape((chunk_rows - relay_rows, tok_rows), BF16)
    chunk_flops = 2 * chunk_rows * tok_rows * features
    block = call(
        pack_kernel,
        (passing_rows, wk, wv, flat(anchor_keys), flat(anchor_values)),
        row(packed),
        4 * retained * tok_rows * size,
        in_specs=[HBM] * 5,
        scratch=[
            pltpu.VMEM(passing_rows.shape, jnp.int32),
            pltpu.VMEM((tok_rows, size), BF16),
            pltpu.VMEM((tok_rows, size), BF16),
            DMA((5,)),
        ],
    )
    query_rows = heads * tok_rows
    stats = (
        shape((1, query_rows), F32),
        shape((1, query_rows), F32),
        shape((size, query_rows), F32),
    )
    qh, hide, w_farther, *state = call(
        own_kernel,
        (block_of_device, queries.reshape(query_rows, size), wk, wv, out_weight),
        (row(query_rows), shape((slots, tok_rows), F32), weight, *stats),
        4 * query_rows * tok_rows * size,
        in_specs=[HBM] * 5,
        scratch=[
            pltpu.SMEM((slots,), jnp.int32),
            pltpu.VMEM((query_rows, size), BF16),
            pltpu.VMEM((tok_rows, size), BF16),
            pltpu.VMEM((tok_rows, size), BF16),
            pltpu.VMEM((query_rows, size), F32),
            DMA((4 + PARTS,)),
        ],
    )
    order = [0]
    step = slots // 2
    held = block

    def exchange(mask):
        return lax.ppermute(held, "ctx", [(i, i ^ mask) for i in range(slots)])

    while step > 4:
        held = jnp.concatenate([held, exchange(step)], axis=0)
        order = order + [j ^ step for j in order]
        step //= 2
    masks = (6, 4, 2)
    held = jnp.concatenate([held] + [exchange(mask) for mask in masks], axis=0)
    order = [j ^ mask for mask in (0, *masks) for j in order]
    w_far, w_near = call(
        fetch_kernel, (hide, out_weight), (weight, weight), 0, in_specs=[VMEM, HBM], scratch=[DMA((2 * PARTS,))]
    )
    step = 1
    other = exchange(step)
    late_order = [j ^ step for j in order]
    half = (slots // 2, packed, size)
    fold_flops = 4 * query_rows * (slots // 2) * (anchors + retained) * size
    state = call(
        functools.partial(early_kernel, order, anchors, retained),
        (qh, hide, held.reshape(half), *state),
        stats,
        fold_flops,
    )
    att, first = call(
        functools.partial(late_kernel, late_order, anchors, retained),
        (qh, hide, other.reshape(half), *state, w_farther),
        (shape((features, tok_rows), BF16), relayed),
        fold_flops + chunk_flops // 2,
    )

    def send(x, mask):
        return lax.ppermute(x, "tp", [(i, i ^ mask) for i in range(tp)])

    relay = send(first, 1)
    farther, far = call(direct_kernel, (att, w_farther, w_far), (direct, direct), chunk_flops)
    farther = send(farther, 3)
    far = send(far, 2)
    across, near = call(later_kernel, (att, w_far, w_near), (relayed, chunk), chunk_flops)
    across = send(add(across, relay), 2)
    near = send(near, 1)
    own = call(
        own_chunk_kernel,
        (att, out_weight),
        chunk,
        chunk_flops,
        in_specs=[VMEM, HBM],
        scratch=[pltpu.VMEM((chunk_rows, features), BF16), DMA((PARTS,))],
    )
    top = add(own[:relay_rows], near[:relay_rows], across)
    low = add(own[relay_rows:], near[relay_rows:], far, farther)
    return jnp.concatenate([top, low], axis=0)


def solution(mesh):
    placed = (
        P("ctx", "tp", None),
        P("ctx", "tp", None),
        P("ctx", "tp", None),
        P("ctx", "tp", None),
        P("ctx", "tp", None),
        P(),
        P(),
        P(None, "tp"),
    )
    return jax.shard_map(layer, mesh=mesh, in_specs=placed, out_specs=P("tp", "ctx"), check_vma=False)
```

```python
import functools
import math

import jax
import jax.numpy as jnp
from jax import lax
from jax.experimental import pallas as pl
from jax.experimental.pallas import tpu as pltpu
from jax.sharding import PartitionSpec as P


BF16 = jnp.bfloat16
F32 = jnp.float32
HIDDEN = -1e30
VMEM = pl.BlockSpec(memory_space=pltpu.VMEM)
HBM = pl.BlockSpec(memory_space=pltpu.HBM)
DMA = pltpu.SemaphoreType.DMA
PAIR = 2
PARTS = 4
RELAY_PARTS, ALL_PARTS = 5, 8


def dot(a, b, a_dim, b_dim):
    return lax.dot_general(a, b, (((a_dim,), (b_dim,)), ((), ())), preferred_element_type=F32)


def call(kernel, inputs, out_shape, flops, in_specs=None, scratch=()):
    if in_specs:
        inputs = [pltpu.with_memory_space_constraint(x, pltpu.HBM) if s is HBM else x for x, s in zip(inputs, in_specs)]
    moved = sum(x.size * x.dtype.itemsize for x in inputs)
    return pl.pallas_call(
        kernel,
        out_shape=out_shape,
        in_specs=in_specs or [VMEM] * len(inputs),
        out_specs=jax.tree.map(lambda _: VMEM, out_shape),
        scratch_shapes=scratch,
        compiler_params=pltpu.CompilerParams(vmem_limit_bytes=32 << 20),
        cost_estimate=pl.CostEstimate(flops=flops, bytes_accessed=moved, transcendentals=0),
    )(*inputs)


def fetch(pairs, sems):
    copies = [pltpu.make_async_copy(a, b, sems.at[i]) for i, (a, b) in enumerate(pairs)]
    for copy in copies:
        copy.start()
    return copies


def wait(copies):
    for copy in copies:
        copy.wait()


def pack_kernel(rows_hbm, wk_hbm, wv_hbm, ak_hbm, av_hbm, out_ref, rows_ref, wk_ref, wv_ref, sems):
    anchors, retained = ak_hbm.shape[0], rows_ref.shape[1]
    first = 2 * anchors
    pairs = [
        (rows_hbm, rows_ref),
        (wk_hbm, wk_ref),
        (wv_hbm, wv_ref),
        (ak_hbm, out_ref.at[0:anchors, :]),
        (av_hbm, out_ref.at[anchors:first, :]),
    ]
    wait(fetch(pairs, sems))
    slot = lax.axis_index("ctx")
    chosen = rows_ref[pl.ds(slot, 1), :]
    places = lax.broadcasted_iota(jnp.int32, (wk_ref.shape[0], retained), 0)
    one_hot = (places == chosen).astype(BF16)
    out_ref[first : first + retained, :] = dot(one_hot, wk_ref[...], 0, 0).astype(BF16)
    out_ref[first + retained :, :] = dot(one_hot, wv_ref[...], 0, 0).astype(BF16)


def fold(q, before, groups, value_cols, factor):
    scores = jnp.concatenate([mask(dot(keys, q, 1, 1)) for keys, mask in groups], axis=0)
    top = jnp.max(scores, axis=0, keepdims=True)
    if before is not None:
        top = jnp.maximum(top, before[0])
    weights = jnp.exp2((scores - top) * factor)
    total = jnp.sum(weights, axis=0, keepdims=True)
    summed = dot(value_cols, weights.astype(BF16), 1, 0)
    if before is not None:
        fade = jnp.exp2((before[0] - top) * factor)
        total = total + before[1] * fade
        summed = summed + before[2] * fade
    return top, total, summed


def factor_of(size):
    return size ** (-0.5) * math.log2(math.e)


def parts_of(w_hbm, mask, first, w_ref):
    rows = w_ref.shape[0]
    begin = (lax.axis_index("tp") ^ mask) * (w_hbm.shape[0] // lax.axis_size("tp")) + first
    part = rows // PARTS
    return [
        (w_hbm.at[pl.ds(pl.multiple_of(begin + i, 16), part), :], w_ref.at[i : i + part, :])
        for i in range(0, rows, part)
    ]


def own_kernel(blocks_hbm, q_hbm, wk_hbm, wv_hbm, w_hbm,
               qh_ref, hide_ref, farther_ref, far_ref, top_ref, total_ref, summed_ref,
               blocks_ref, q_ref, wk_ref, wv_ref, qf_ref, sems):
    pairs = [(blocks_hbm, blocks_ref), (q_hbm, q_ref), (wk_hbm, wk_ref), (wv_hbm, wv_ref)]
    weights = parts_of(w_hbm, 3, 0, farther_ref)
    weights += parts_of(w_hbm, 2, farther_ref.shape[0] - far_ref.shape[0], far_ref)
    copies = fetch(pairs + weights, sems)
    wait(copies[: len(pairs)])
    tok_rows, size = wk_ref.shape
    heads = q_ref.shape[0] // tok_rows
    slot = lax.axis_index("ctx")
    own_block = blocks_ref[slot]
    for j in range(blocks_ref.shape[0]):
        bias = jnp.where(blocks_ref[slot ^ j] < own_block, 0.0, HIDDEN)
        hide_ref[j : j + 1, :] = jnp.full((1, hide_ref.shape[1]), bias, F32)
    qf_ref[...] = q_ref[...].astype(F32)
    lanes = PAIR * tok_rows
    key_at = lax.broadcasted_iota(jnp.int32, (tok_rows, lanes), 0)
    row_at = lax.broadcasted_iota(jnp.int32, (tok_rows, lanes), 1) % tok_rows
    causal = key_at <= row_at
    value_cols = wv_ref[...].T
    for h in range(0, heads, PAIR):
        for j in range(h, h + PAIR):
            qh_ref[j * tok_rows : (j + 1) * tok_rows, :] = qf_ref[
                pl.ds(j, tok_rows, stride=heads), :
            ].astype(BF16)
        cols = slice(h * tok_rows, (h + PAIR) * tok_rows)
        groups = [(wk_ref[...], lambda s: jnp.where(causal, s, HIDDEN))]
        state = fold(qh_ref[cols, :], None, groups, value_cols, factor_of(size))
        top_ref[:, cols], total_ref[:, cols], summed_ref[:, cols] = state
    wait(copies[len(pairs) :])


def rows_of(block_ref, anchors, retained):
    slots, _, size = block_ref.shape
    first = 2 * anchors
    take = lambda a, n: block_ref[:, a : a + n, :].reshape(slots * n, size)
    seen, past = take(0, anchors), take(first, retained)
    values = jnp.concatenate([take(anchors, anchors), take(first + retained, retained)], axis=0)
    return seen, past, values.T


def hidden_rows(hide_ref, order, retained, lanes):
    width = hide_ref.shape[1]
    rows = [jnp.broadcast_to(hide_ref[j : j + 1, :], (retained, width)) for j in order]
    column = jnp.concatenate(rows, axis=0)
    return jnp.concatenate([column] * (lanes // width), axis=1)


def fold_blocks(orders, anchors, retained, qh_ref, hide_ref, block_refs, state_refs, finish):
    top_ref, total_ref, summed_ref = state_refs
    tok_rows = hide_ref.shape[1]
    size = qh_ref.shape[1]
    heads = qh_ref.shape[0] // tok_rows
    groups, columns = [], []
    for order, block_ref in zip(orders, block_refs):
        seen, past, value_cols = rows_of(block_ref, anchors, retained)
        bias = hidden_rows(hide_ref, order, retained, PAIR * tok_rows)
        groups += [(seen, lambda s: s), (past, lambda s, bias=bias: s + bias)]
        columns.append(value_cols)
    value_cols = jnp.concatenate(columns, axis=1)
    for h in range(0, heads, PAIR):
        cols = slice(h * tok_rows, (h + PAIR) * tok_rows)
        before = (top_ref[:, cols], total_ref[:, cols], summed_ref[:, cols])
        finish(h, cols, fold(qh_ref[cols, :], before, groups, value_cols, factor_of(size)))


def early_kernel(orders, anchors, retained, qh_ref, hide_ref, *refs):
    block_refs, (top0, total0, summed0, top_ref, total_ref, summed_ref) = refs[: len(orders)], refs[len(orders) :]

    def finish(h, cols, state):
        top_ref[:, cols], total_ref[:, cols], summed_ref[:, cols] = state

    fold_blocks(orders, anchors, retained, qh_ref, hide_ref, block_refs, (top0, total0, summed0), finish)


def project(w_ref, first, att_ref, out_ref):
    rows = out_ref.shape[0]
    tile = math.gcd(256, rows)
    for start in range(0, rows, tile):
        part = dot(w_ref[first + start : first + start + tile, :], att_ref[...], 1, 0)
        out_ref[start : start + tile, :] = part.astype(out_ref.dtype)


def late_kernel(orders, anchors, retained, qh_ref, hide_ref, block_ref, top0, total0, summed0, w_ref,
                att_ref, first_ref):
    tok_rows = hide_ref.shape[1]
    size = qh_ref.shape[1]

    def finish(h, cols, state):
        _, total, summed = state
        attended = (summed / total).astype(BF16)
        for j in range(PAIR):
            att_ref[(h + j) * size : (h + j + 1) * size, :] = attended[:, j * tok_rows : (j + 1) * tok_rows]

    fold_blocks(orders, anchors, retained, qh_ref, hide_ref, (block_ref,), (top0, total0, summed0), finish)
    project(w_ref, 0, att_ref, first_ref)


def direct_kernel(att_ref, farther_w, far_w, far_ref, farther_ref):
    project(far_w, 0, att_ref, far_ref)
    project(farther_w, farther_w.shape[0] - farther_ref.shape[0], att_ref, farther_ref)


def later_kernel(att_ref, w_hbm, across_ref, near_ref, far_w, near_w, sems):
    copies = fetch(parts_of(w_hbm, 2, 0, far_w) + parts_of(w_hbm, 1, 0, near_w), sems)
    wait(copies)
    project(far_w, 0, att_ref, across_ref)
    project(near_w, 0, att_ref, near_ref)


def own_chunk_kernel(att_ref, w_hbm, out_ref, w_ref, sems):
    wait(fetch(parts_of(w_hbm, 0, 0, w_ref), sems))
    project(w_ref, 0, att_ref, out_ref)


def add(*parts):
    return functools.reduce(jnp.add, [p.astype(F32) for p in parts]).astype(BF16)


def layer(queries, window_keys, window_values, anchor_keys, anchor_values, passing_rows, block_of_device, out_weight):
    tok_rows, heads, size = queries.shape
    anchors, retained = anchor_keys.shape[0], passing_rows.shape[1]
    slots = block_of_device.shape[0]
    flat = lambda x: x.reshape(x.shape[0], size)
    wk, wv = flat(window_keys), flat(window_values)
    packed = 2 * (anchors + retained)
    shape = jax.ShapeDtypeStruct
    tp = lax.axis_size("tp")
    chunk_rows = out_weight.shape[0] // tp
    features = heads * size
    row = lambda n: shape((n, size), BF16)
    chunk = shape((chunk_rows, tok_rows), BF16)
    weights = lambda n: shape((n, features), BF16)
    relay_rows = chunk_rows * RELAY_PARTS // ALL_PARTS
    relayed = shape((relay_rows, tok_rows), BF16)
    direct = shape((chunk_rows - relay_rows, tok_rows), BF16)
    chunk_flops = 2 * chunk_rows * tok_rows * features
    block = call(
        pack_kernel,
        (passing_rows, wk, wv, flat(anchor_keys), flat(anchor_values)),
        row(packed),
        4 * retained * tok_rows * size,
        in_specs=[HBM] * 5,
        scratch=[
            pltpu.VMEM(passing_rows.shape, jnp.int32),
            pltpu.VMEM((tok_rows, size), BF16),
            pltpu.VMEM((tok_rows, size), BF16),
            DMA((5,)),
        ],
    )
    query_rows = heads * tok_rows
    stats = (
        shape((1, query_rows), F32),
        shape((1, query_rows), F32),
        shape((size, query_rows), F32),
    )
    qh, hide, w_farther, w_far, *state = call(
        own_kernel,
        (block_of_device, queries.reshape(query_rows, size), wk, wv, out_weight),
        (row(query_rows), shape((slots, tok_rows), F32), weights(chunk_rows), weights(chunk_rows - relay_rows), *stats),
        4 * query_rows * tok_rows * size,
        in_specs=[HBM] * 5,
        scratch=[
            pltpu.SMEM((slots,), jnp.int32),
            pltpu.VMEM((query_rows, size), BF16),
            pltpu.VMEM((tok_rows, size), BF16),
            pltpu.VMEM((tok_rows, size), BF16),
            pltpu.VMEM((query_rows, size), F32),
            DMA((4 + 2 * PARTS,)),
        ],
    )
    order = [0]
    step = slots // 2
    held = block

    def exchange(mask):
        return lax.ppermute(held, "ctx", [(i, i ^ mask) for i in range(slots)])

    while step > 4:
        held = jnp.concatenate([held, exchange(step)], axis=0)
        order = order + [j ^ step for j in order]
        step //= 2
    pieces = [exchange(mask) for mask in (6, 4, 2)]
    partner = exchange(1)
    partner_order = [j ^ 1 for j in order]
    rest_order = [j ^ mask for mask in (6, 4, 2) for j in order]
    late_order = [j ^ 1 for j in rest_order]
    blocks = lambda x: x.reshape(x.shape[0] // packed, packed, size)
    fold_flops = lambda n: 4 * query_rows * n * (anchors + retained) * size
    state = call(
        functools.partial(early_kernel, (order, partner_order), anchors, retained),
        (qh, hide, blocks(held), blocks(partner), *state),
        stats,
        fold_flops(2 * len(order)),
    )
    held = jnp.concatenate(pieces, axis=0)
    other = exchange(1)
    state = call(
        functools.partial(early_kernel, (rest_order,), anchors, retained),
        (qh, hide, blocks(held), *state),
        stats,
        fold_flops(len(rest_order)),
    )
    att, first = call(
        functools.partial(late_kernel, (late_order,), anchors, retained),
        (qh, hide, blocks(other), *state, w_farther),
        (shape((features, tok_rows), BF16), relayed),
        fold_flops(len(late_order)) + chunk_flops // 2,
    )

    def send(x, mask):
        return lax.ppermute(x, "tp", [(i, i ^ mask) for i in range(tp)])

    relay = send(first, 1)
    far, farther = call(direct_kernel, (att, w_farther, w_far), (direct, direct), chunk_flops)
    far = send(far, 2)
    farther = send(farther, 3)
    across, near = call(
        later_kernel,
        (att, out_weight),
        (relayed, chunk),
        chunk_flops,
        in_specs=[VMEM, HBM],
        scratch=[pltpu.VMEM((relay_rows, features), BF16), pltpu.VMEM((chunk_rows, features), BF16), DMA((2 * PARTS,))],
    )
    across = send(add(across, relay), 2)
    near = send(near, 1)
    own = call(
        own_chunk_kernel,
        (att, out_weight),
        chunk,
        chunk_flops,
        in_specs=[VMEM, HBM],
        scratch=[pltpu.VMEM((chunk_rows, features), BF16), DMA((PARTS,))],
    )
    top = add(own[:relay_rows], near[:relay_rows], across)
    low = add(own[relay_rows:], near[relay_rows:], far, farther)
    return jnp.concatenate([top, low], axis=0)


def solution(mesh):
    placed = (
        P("ctx", "tp", None),
        P("ctx", "tp", None),
        P("ctx", "tp", None),
        P("ctx", "tp", None),
        P("ctx", "tp", None),
        P(),
        P(),
        P(None, "tp"),
    )
    return jax.shard_map(layer, mesh=mesh, in_specs=placed, out_specs=P("tp", "ctx"), check_vma=False)
```

```python
import functools
import math

import jax
import jax.numpy as jnp
from jax import lax
from jax.experimental import pallas as pl
from jax.experimental.pallas import tpu as pltpu
from jax.sharding import PartitionSpec as P


BF16 = jnp.bfloat16
F32 = jnp.float32
HIDDEN = -1e30
VMEM = pl.BlockSpec(memory_space=pltpu.VMEM)
HBM = pl.BlockSpec(memory_space=pltpu.HBM)
DMA = pltpu.SemaphoreType.DMA
GROUP = 8
PARTS = 4
RELAY_PARTS, ALL_PARTS = 5, 8


def dot(a, b, a_dim, b_dim):
    return lax.dot_general(a, b, (((a_dim,), (b_dim,)), ((), ())), preferred_element_type=F32)


def call(kernel, inputs, out_shape, flops, in_specs=None, scratch=()):
    if in_specs:
        inputs = [pltpu.with_memory_space_constraint(x, pltpu.HBM) if s is HBM else x for x, s in zip(inputs, in_specs)]
    moved = sum(x.size * x.dtype.itemsize for x in inputs)
    return pl.pallas_call(
        kernel,
        out_shape=out_shape,
        in_specs=in_specs or [VMEM] * len(inputs),
        out_specs=jax.tree.map(lambda _: VMEM, out_shape),
        scratch_shapes=scratch,
        compiler_params=pltpu.CompilerParams(vmem_limit_bytes=32 << 20),
        cost_estimate=pl.CostEstimate(flops=flops, bytes_accessed=moved, transcendentals=0),
    )(*inputs)


def fetch(pairs, sems):
    copies = [pltpu.make_async_copy(a, b, sems.at[i]) for i, (a, b) in enumerate(pairs)]
    for copy in copies:
        copy.start()
    return copies


def wait(copies):
    for copy in copies:
        copy.wait()


def pack_kernel(rows_hbm, wk_hbm, wv_hbm, ak_hbm, av_hbm, out_ref, rows_ref, wk_ref, wv_ref, sems):
    anchors, retained = ak_hbm.shape[0], rows_ref.shape[1]
    first = 2 * anchors
    pairs = [
        (rows_hbm, rows_ref),
        (wk_hbm, wk_ref),
        (wv_hbm, wv_ref),
        (ak_hbm, out_ref.at[0:anchors, :]),
        (av_hbm, out_ref.at[anchors:first, :]),
    ]
    wait(fetch(pairs, sems))
    slot = lax.axis_index("ctx")
    chosen = rows_ref[pl.ds(slot, 1), :]
    places = lax.broadcasted_iota(jnp.int32, (wk_ref.shape[0], retained), 0)
    one_hot = (places == chosen).astype(BF16)
    out_ref[first : first + retained, :] = dot(one_hot, wk_ref[...], 0, 0).astype(BF16)
    out_ref[first + retained :, :] = dot(one_hot, wv_ref[...], 0, 0).astype(BF16)


def fold(q, before, groups, value_cols, factor):
    scores = jnp.concatenate([mask(dot(keys, q, 1, 1)) for keys, mask in groups], axis=0)
    top = jnp.max(scores, axis=0, keepdims=True)
    if before is not None:
        top = jnp.maximum(top, before[0])
    weights = jnp.exp2((scores - top) * factor)
    total = jnp.sum(weights, axis=0, keepdims=True)
    summed = dot(value_cols, weights.astype(BF16), 1, 0)
    if before is not None:
        fade = jnp.exp2((before[0] - top) * factor)
        total = total + before[1] * fade
        summed = summed + before[2] * fade
    return top, total, summed


def factor_of(size):
    return size ** (-0.5) * math.log2(math.e)


def parts_of(w_hbm, mask, first, w_ref):
    rows = w_ref.shape[0]
    begin = (lax.axis_index("tp") ^ mask) * (w_hbm.shape[0] // lax.axis_size("tp")) + first
    part = rows // PARTS
    return [
        (w_hbm.at[pl.ds(pl.multiple_of(begin + i, 16), part), :], w_ref.at[i : i + part, :])
        for i in range(0, rows, part)
    ]


def own_kernel(blocks_hbm, q_hbm, wk_hbm, wv_hbm, w_hbm,
               qh_ref, hide_ref, farther_ref, far_ref, top_ref, total_ref, summed_ref,
               blocks_ref, q_ref, wk_ref, wv_ref, qf_ref, sems):
    pairs = [(blocks_hbm, blocks_ref), (q_hbm, q_ref), (wk_hbm, wk_ref), (wv_hbm, wv_ref)]
    weights = parts_of(w_hbm, 3, 0, farther_ref)
    weights += parts_of(w_hbm, 2, farther_ref.shape[0] - far_ref.shape[0], far_ref)
    copies = fetch(pairs + weights, sems)
    wait(copies[: len(pairs)])
    tok_rows, size = wk_ref.shape
    heads = q_ref.shape[0] // tok_rows
    slot = lax.axis_index("ctx")
    own_block = blocks_ref[slot]
    for j in range(blocks_ref.shape[0]):
        bias = jnp.where(blocks_ref[slot ^ j] < own_block, 0.0, HIDDEN)
        hide_ref[j : j + 1, :] = jnp.full((1, hide_ref.shape[1]), bias, F32)
    qf_ref[...] = q_ref[...].astype(F32)
    lanes = GROUP * tok_rows
    key_at = lax.broadcasted_iota(jnp.int32, (tok_rows, lanes), 0)
    row_at = lax.broadcasted_iota(jnp.int32, (tok_rows, lanes), 1) % tok_rows
    causal = key_at <= row_at
    value_cols = wv_ref[...].T
    for h in range(0, heads, GROUP):
        for j in range(h, h + GROUP):
            qh_ref[j * tok_rows : (j + 1) * tok_rows, :] = qf_ref[
                pl.ds(j, tok_rows, stride=heads), :
            ].astype(BF16)
        cols = slice(h * tok_rows, (h + GROUP) * tok_rows)
        groups = [(wk_ref[...], lambda s: jnp.where(causal, s, HIDDEN))]
        state = fold(qh_ref[cols, :], None, groups, value_cols, factor_of(size))
        top_ref[:, cols], total_ref[:, cols], summed_ref[:, cols] = state
    wait(copies[len(pairs) :])


def rows_of(block_ref, anchors, retained):
    slots, _, size = block_ref.shape
    first = 2 * anchors
    take = lambda a, n: block_ref[:, a : a + n, :].reshape(slots * n, size)
    seen, past = take(0, anchors), take(first, retained)
    values = jnp.concatenate([take(anchors, anchors), take(first + retained, retained)], axis=0)
    return seen, past, values.T


def hidden_rows(hide_ref, order, retained, lanes):
    width = hide_ref.shape[1]
    rows = [jnp.broadcast_to(hide_ref[j : j + 1, :], (retained, width)) for j in order]
    column = jnp.concatenate(rows, axis=0)
    return jnp.concatenate([column] * (lanes // width), axis=1)


def fold_blocks(orders, anchors, retained, qh_ref, hide_ref, block_refs, state_refs, finish):
    top_ref, total_ref, summed_ref = state_refs
    tok_rows = hide_ref.shape[1]
    size = qh_ref.shape[1]
    heads = qh_ref.shape[0] // tok_rows
    groups, columns = [], []
    for order, block_ref in zip(orders, block_refs):
        seen, past, value_cols = rows_of(block_ref, anchors, retained)
        bias = hidden_rows(hide_ref, order, retained, GROUP * tok_rows)
        groups += [(seen, lambda s: s), (past, lambda s, bias=bias: s + bias)]
        columns.append(value_cols)
    value_cols = jnp.concatenate(columns, axis=1)
    for h in range(0, heads, GROUP):
        cols = slice(h * tok_rows, (h + GROUP) * tok_rows)
        before = (top_ref[:, cols], total_ref[:, cols], summed_ref[:, cols])
        finish(h, cols, fold(qh_ref[cols, :], before, groups, value_cols, factor_of(size)))


def early_kernel(orders, anchors, retained, qh_ref, hide_ref, *refs):
    block_refs, (top0, total0, summed0, top_ref, total_ref, summed_ref) = refs[: len(orders)], refs[len(orders) :]

    def finish(h, cols, state):
        top_ref[:, cols], total_ref[:, cols], summed_ref[:, cols] = state

    fold_blocks(orders, anchors, retained, qh_ref, hide_ref, block_refs, (top0, total0, summed0), finish)


def project(w_ref, first, att_ref, out_ref):
    rows = out_ref.shape[0]
    tile = math.gcd(256, rows)
    for start in range(0, rows, tile):
        part = dot(w_ref[first + start : first + start + tile, :], att_ref[...], 1, 0)
        out_ref[start : start + tile, :] = part.astype(out_ref.dtype)


def late_kernel(orders, anchors, retained, qh_ref, hide_ref, block_ref, top0, total0, summed0, w_ref, far_w,
                att_ref, first_ref, far_ref):
    tok_rows = hide_ref.shape[1]
    size = qh_ref.shape[1]

    def finish(h, cols, state):
        _, total, summed = state
        attended = (summed / total).astype(BF16)
        for j in range(GROUP):
            att_ref[(h + j) * size : (h + j + 1) * size, :] = attended[:, j * tok_rows : (j + 1) * tok_rows]

    fold_blocks(orders, anchors, retained, qh_ref, hide_ref, (block_ref,), (top0, total0, summed0), finish)
    project(w_ref, 0, att_ref, first_ref)
    project(far_w, 0, att_ref, far_ref)


def direct_kernel(att_ref, farther_w, farther_ref):
    project(farther_w, farther_w.shape[0] - farther_ref.shape[0], att_ref, farther_ref)


def later_kernel(att_ref, w_hbm, across_ref, near_ref, far_w, near_w, sems):
    copies = fetch(parts_of(w_hbm, 2, 0, far_w) + parts_of(w_hbm, 1, 0, near_w), sems)
    wait(copies)
    project(far_w, 0, att_ref, across_ref)
    project(near_w, 0, att_ref, near_ref)


def own_chunk_kernel(att_ref, w_hbm, out_ref, w_ref, sems):
    wait(fetch(parts_of(w_hbm, 0, 0, w_ref), sems))
    project(w_ref, 0, att_ref, out_ref)


def add(*parts):
    return functools.reduce(jnp.add, [p.astype(F32) for p in parts]).astype(BF16)


def layer(queries, window_keys, window_values, anchor_keys, anchor_values, passing_rows, block_of_device, out_weight):
    tok_rows, heads, size = queries.shape
    anchors, retained = anchor_keys.shape[0], passing_rows.shape[1]
    slots = block_of_device.shape[0]
    flat = lambda x: x.reshape(x.shape[0], size)
    wk, wv = flat(window_keys), flat(window_values)
    packed = 2 * (anchors + retained)
    shape = jax.ShapeDtypeStruct
    tp = lax.axis_size("tp")
    chunk_rows = out_weight.shape[0] // tp
    features = heads * size
    row = lambda n: shape((n, size), BF16)
    chunk = shape((chunk_rows, tok_rows), BF16)
    weights = lambda n: shape((n, features), BF16)
    relay_rows = chunk_rows * RELAY_PARTS // ALL_PARTS
    relayed = shape((relay_rows, tok_rows), BF16)
    direct = shape((chunk_rows - relay_rows, tok_rows), BF16)
    chunk_flops = 2 * chunk_rows * tok_rows * features
    block = call(
        pack_kernel,
        (passing_rows, wk, wv, flat(anchor_keys), flat(anchor_values)),
        row(packed),
        4 * retained * tok_rows * size,
        in_specs=[HBM] * 5,
        scratch=[
            pltpu.VMEM(passing_rows.shape, jnp.int32),
            pltpu.VMEM((tok_rows, size), BF16),
            pltpu.VMEM((tok_rows, size), BF16),
            DMA((5,)),
        ],
    )
    query_rows = heads * tok_rows
    stats = (
        shape((1, query_rows), F32),
        shape((1, query_rows), F32),
        shape((size, query_rows), F32),
    )
    qh, hide, w_farther, w_far, *state = call(
        own_kernel,
        (block_of_device, queries.reshape(query_rows, size), wk, wv, out_weight),
        (row(query_rows), shape((slots, tok_rows), F32), weights(chunk_rows), weights(chunk_rows - relay_rows), *stats),
        4 * query_rows * tok_rows * size,
        in_specs=[HBM] * 5,
        scratch=[
            pltpu.SMEM((slots,), jnp.int32),
            pltpu.VMEM((query_rows, size), BF16),
            pltpu.VMEM((tok_rows, size), BF16),
            pltpu.VMEM((tok_rows, size), BF16),
            pltpu.VMEM((query_rows, size), F32),
            DMA((4 + 2 * PARTS,)),
        ],
    )
    order = [0]
    step = slots // 2
    held = block

    def exchange(mask):
        return lax.ppermute(held, "ctx", [(i, i ^ mask) for i in range(slots)])

    while step > 4:
        held = jnp.concatenate([held, exchange(step)], axis=0)
        order = order + [j ^ step for j in order]
        step //= 2
    diagonal, *sides = [exchange(mask) for mask in (6, 4, 2)]
    partner = exchange(1)
    across_chip = lambda order, mask: [j ^ mask for j in order]
    partner_order, diagonal_order = across_chip(order, 1), across_chip(order, 6)
    side_order = across_chip(order, 4) + across_chip(order, 2)
    blocks = lambda x: x.reshape(x.shape[0] // packed, packed, size)
    fold_flops = lambda n: 4 * query_rows * n * (anchors + retained) * size

    def attend(state, *pairs):
        orders, arrays = zip(*pairs)
        return call(
            functools.partial(early_kernel, orders, anchors, retained),
            (qh, hide, *[blocks(x) for x in arrays], *state),
            stats,
            fold_flops(sum(len(o) for o in orders)),
        )

    own_held, held = held, diagonal
    diagonal_partner = exchange(1)
    state = attend(state, (order, own_held), (partner_order, partner), (diagonal_order, diagonal))
    held = jnp.concatenate(sides, axis=0)
    other = exchange(1)
    state = attend(state, (across_chip(diagonal_order, 1), diagonal_partner), (side_order, held))
    late_order = across_chip(side_order, 1)
    att, first, far = call(
        functools.partial(late_kernel, (late_order,), anchors, retained),
        (qh, hide, blocks(other), *state, w_farther, w_far),
        (shape((features, tok_rows), BF16), relayed, direct),
        fold_flops(len(late_order)) + chunk_flops // 2,
    )

    def send(x, mask):
        return lax.ppermute(x, "tp", [(i, i ^ mask) for i in range(tp)])

    relay = send(first, 1)
    farther = call(direct_kernel, (att, w_farther), direct, chunk_flops)
    far = send(far, 2)
    farther = send(farther, 3)
    across, near = call(
        later_kernel,
        (att, out_weight),
        (relayed, chunk),
        chunk_flops,
        in_specs=[VMEM, HBM],
        scratch=[pltpu.VMEM((relay_rows, features), BF16), pltpu.VMEM((chunk_rows, features), BF16), DMA((2 * PARTS,))],
    )
    across = send(add(across, relay), 2)
    near = send(near, 1)
    own = call(
        own_chunk_kernel,
        (att, out_weight),
        chunk,
        chunk_flops,
        in_specs=[VMEM, HBM],
        scratch=[pltpu.VMEM((chunk_rows, features), BF16), DMA((PARTS,))],
    )
    top = add(own[:relay_rows], near[:relay_rows], across)
    low = add(own[relay_rows:], near[relay_rows:], far, farther)
    return jnp.concatenate([top, low], axis=0)


def solution(mesh):
    placed = (
        P("ctx", "tp", None),
        P("ctx", "tp", None),
        P("ctx", "tp", None),
        P("ctx", "tp", None),
        P("ctx", "tp", None),
        P(),
        P(),
        P(None, "tp"),
    )
    return jax.shard_map(layer, mesh=mesh, in_specs=placed, out_specs=P("tp", "ctx"), check_vma=False)
```

```python
import functools
import math

import jax
import jax.numpy as jnp
from jax import lax
from jax.experimental import pallas as pl
from jax.experimental.pallas import tpu as pltpu
from jax.sharding import PartitionSpec as P


BF16 = jnp.bfloat16
F32 = jnp.float32
HIDDEN = -1e30
VMEM = pl.BlockSpec(memory_space=pltpu.VMEM)
HBM = pl.BlockSpec(memory_space=pltpu.HBM)
DMA = pltpu.SemaphoreType.DMA
GROUP = 8
PARTS = 4
RELAY_PARTS, ALL_PARTS = 10, 16


def dot(a, b, a_dim, b_dim):
    return lax.dot_general(a, b, (((a_dim,), (b_dim,)), ((), ())), preferred_element_type=F32)


def call(kernel, inputs, out_shape, flops, in_specs=None, scratch=()):
    if in_specs:
        inputs = [pltpu.with_memory_space_constraint(x, pltpu.HBM) if s is HBM else x for x, s in zip(inputs, in_specs)]
    moved = sum(x.size * x.dtype.itemsize for x in inputs)
    return pl.pallas_call(
        kernel,
        out_shape=out_shape,
        in_specs=in_specs or [VMEM] * len(inputs),
        out_specs=jax.tree.map(lambda _: VMEM, out_shape),
        scratch_shapes=scratch,
        compiler_params=pltpu.CompilerParams(vmem_limit_bytes=32 << 20),
        cost_estimate=pl.CostEstimate(flops=flops, bytes_accessed=moved, transcendentals=0),
    )(*inputs)


def fetch(pairs, sems):
    copies = [pltpu.make_async_copy(a, b, sems.at[i]) for i, (a, b) in enumerate(pairs)]
    for copy in copies:
        copy.start()
    return copies


def wait(copies):
    for copy in copies:
        copy.wait()


def pack_kernel(rows_hbm, wk_hbm, wv_hbm, ak_hbm, av_hbm, out_ref, rows_ref, wk_ref, wv_ref, sems):
    anchors, retained = ak_hbm.shape[0], rows_ref.shape[1]
    first = 2 * anchors
    pairs = [
        (rows_hbm, rows_ref),
        (wk_hbm, wk_ref),
        (wv_hbm, wv_ref),
        (ak_hbm, out_ref.at[0:anchors, :]),
        (av_hbm, out_ref.at[anchors:first, :]),
    ]
    wait(fetch(pairs, sems))
    slot = lax.axis_index("ctx")
    chosen = rows_ref[pl.ds(slot, 1), :]
    places = lax.broadcasted_iota(jnp.int32, (wk_ref.shape[0], retained), 0)
    one_hot = (places == chosen).astype(BF16)
    out_ref[first : first + retained, :] = dot(one_hot, wk_ref[...], 0, 0).astype(BF16)
    out_ref[first + retained :, :] = dot(one_hot, wv_ref[...], 0, 0).astype(BF16)


def fold(q, before, groups, value_cols, factor):
    scores = jnp.concatenate([mask(dot(keys, q, 1, 1)) for keys, mask in groups], axis=0)
    top = jnp.max(scores, axis=0, keepdims=True)
    if before is not None:
        top = jnp.maximum(top, before[0])
    weights = jnp.exp2((scores - top) * factor)
    total = jnp.sum(weights, axis=0, keepdims=True)
    summed = dot(value_cols, weights.astype(BF16), 1, 0)
    if before is not None:
        fade = jnp.exp2((before[0] - top) * factor)
        total = total + before[1] * fade
        summed = summed + before[2] * fade
    return top, total, summed


def factor_of(size):
    return size ** (-0.5) * math.log2(math.e)


def parts_of(w_hbm, mask, first, w_ref):
    rows = w_ref.shape[0]
    begin = (lax.axis_index("tp") ^ mask) * (w_hbm.shape[0] // lax.axis_size("tp")) + first
    part = rows // PARTS
    return [
        (w_hbm.at[pl.ds(pl.multiple_of(begin + i, 16), part), :], w_ref.at[i : i + part, :])
        for i in range(0, rows, part)
    ]


def own_kernel(blocks_hbm, q_hbm, wk_hbm, wv_hbm, w_hbm,
               qh_ref, hide_ref, farther_ref, far_ref, top_ref, total_ref, summed_ref,
               blocks_ref, q_ref, wk_ref, wv_ref, qf_ref, sems):
    pairs = [(blocks_hbm, blocks_ref), (q_hbm, q_ref), (wk_hbm, wk_ref), (wv_hbm, wv_ref)]
    weights = parts_of(w_hbm, 3, 0, farther_ref)
    weights += parts_of(w_hbm, 2, farther_ref.shape[0] - far_ref.shape[0], far_ref)
    copies = fetch(pairs + weights, sems)
    wait(copies[: len(pairs)])
    tok_rows, size = wk_ref.shape
    heads = q_ref.shape[0] // tok_rows
    slot = lax.axis_index("ctx")
    own_block = blocks_ref[slot]
    for j in range(blocks_ref.shape[0]):
        bias = jnp.where(blocks_ref[slot ^ j] < own_block, 0.0, HIDDEN)
        hide_ref[j : j + 1, :] = jnp.full((1, hide_ref.shape[1]), bias, F32)
    qf_ref[...] = q_ref[...].astype(F32)
    lanes = GROUP * tok_rows
    key_at = lax.broadcasted_iota(jnp.int32, (tok_rows, lanes), 0)
    row_at = lax.broadcasted_iota(jnp.int32, (tok_rows, lanes), 1) % tok_rows
    causal = key_at <= row_at
    value_cols = wv_ref[...].T
    for h in range(0, heads, GROUP):
        for j in range(h, h + GROUP):
            qh_ref[j * tok_rows : (j + 1) * tok_rows, :] = qf_ref[
                pl.ds(j, tok_rows, stride=heads), :
            ].astype(BF16)
        cols = slice(h * tok_rows, (h + GROUP) * tok_rows)
        groups = [(wk_ref[...], lambda s: jnp.where(causal, s, HIDDEN))]
        state = fold(qh_ref[cols, :], None, groups, value_cols, factor_of(size))
        top_ref[:, cols], total_ref[:, cols], summed_ref[:, cols] = state
    wait(copies[len(pairs) :])


def rows_of(block_ref, anchors, retained):
    slots, _, size = block_ref.shape
    first = 2 * anchors
    take = lambda a, n: block_ref[:, a : a + n, :].reshape(slots * n, size)
    seen, past = take(0, anchors), take(first, retained)
    values = jnp.concatenate([take(anchors, anchors), take(first + retained, retained)], axis=0)
    return seen, past, values.T


def hidden_rows(hide_ref, order, retained, lanes):
    width = hide_ref.shape[1]
    rows = [jnp.broadcast_to(hide_ref[j : j + 1, :], (retained, width)) for j in order]
    column = jnp.concatenate(rows, axis=0)
    return jnp.concatenate([column] * (lanes // width), axis=1)


def fold_blocks(orders, anchors, retained, qh_ref, hide_ref, block_refs, state_refs, finish):
    top_ref, total_ref, summed_ref = state_refs
    tok_rows = hide_ref.shape[1]
    size = qh_ref.shape[1]
    heads = qh_ref.shape[0] // tok_rows
    groups, columns = [], []
    for order, block_ref in zip(orders, block_refs):
        seen, past, value_cols = rows_of(block_ref, anchors, retained)
        bias = hidden_rows(hide_ref, order, retained, GROUP * tok_rows)
        groups += [(seen, lambda s: s), (past, lambda s, bias=bias: s + bias)]
        columns.append(value_cols)
    value_cols = jnp.concatenate(columns, axis=1)
    for h in range(0, heads, GROUP):
        cols = slice(h * tok_rows, (h + GROUP) * tok_rows)
        before = (top_ref[:, cols], total_ref[:, cols], summed_ref[:, cols])
        finish(h, cols, fold(qh_ref[cols, :], before, groups, value_cols, factor_of(size)))


def early_kernel(orders, anchors, retained, qh_ref, hide_ref, *refs):
    block_refs, (top0, total0, summed0, top_ref, total_ref, summed_ref) = refs[: len(orders)], refs[len(orders) :]

    def finish(h, cols, state):
        top_ref[:, cols], total_ref[:, cols], summed_ref[:, cols] = state

    fold_blocks(orders, anchors, retained, qh_ref, hide_ref, block_refs, (top0, total0, summed0), finish)


def project(w_ref, first, att_ref, out_ref):
    rows = out_ref.shape[0]
    for start in range(0, rows, 256):
        stop = min(start + 256, rows)
        part = dot(w_ref[first + start : first + stop, :], att_ref[...], 1, 0)
        out_ref[start:stop, :] = part.astype(out_ref.dtype)


def late_kernel(orders, anchors, retained, qh_ref, hide_ref, block_ref, top0, total0, summed0, w_ref, far_w,
                att_ref, first_ref, far_ref):
    tok_rows = hide_ref.shape[1]
    size = qh_ref.shape[1]

    def finish(h, cols, state):
        _, total, summed = state
        attended = (summed / total).astype(BF16)
        for j in range(GROUP):
            att_ref[(h + j) * size : (h + j + 1) * size, :] = attended[:, j * tok_rows : (j + 1) * tok_rows]

    fold_blocks(orders, anchors, retained, qh_ref, hide_ref, (block_ref,), (top0, total0, summed0), finish)
    project(w_ref, 0, att_ref, first_ref)
    project(far_w, 0, att_ref, far_ref)


def direct_kernel(att_ref, farther_w, farther_ref):
    project(farther_w, farther_w.shape[0] - farther_ref.shape[0], att_ref, farther_ref)


def later_kernel(att_ref, w_hbm, across_ref, near_top_ref, near_low_ref, far_w, near_w, sems):
    copies = fetch(parts_of(w_hbm, 2, 0, far_w) + parts_of(w_hbm, 1, 0, near_w), sems)
    wait(copies)
    project(far_w, 0, att_ref, across_ref)
    project(near_w, 0, att_ref, near_top_ref)
    project(near_w, near_top_ref.shape[0], att_ref, near_low_ref)


def own_chunk_kernel(att_ref, w_hbm, out_ref, w_ref, sems):
    wait(fetch(parts_of(w_hbm, 0, 0, w_ref), sems))
    project(w_ref, 0, att_ref, out_ref)


def add(*parts):
    return functools.reduce(jnp.add, [p.astype(F32) for p in parts]).astype(BF16)


def layer(queries, window_keys, window_values, anchor_keys, anchor_values, passing_rows, block_of_device, out_weight):
    tok_rows, heads, size = queries.shape
    anchors, retained = anchor_keys.shape[0], passing_rows.shape[1]
    slots = block_of_device.shape[0]
    flat = lambda x: x.reshape(x.shape[0], size)
    wk, wv = flat(window_keys), flat(window_values)
    packed = 2 * (anchors + retained)
    shape = jax.ShapeDtypeStruct
    tp = lax.axis_size("tp")
    chunk_rows = out_weight.shape[0] // tp
    features = heads * size
    row = lambda n: shape((n, size), BF16)
    chunk = shape((chunk_rows, tok_rows), BF16)
    weights = lambda n: shape((n, features), BF16)
    relay_rows = chunk_rows * RELAY_PARTS // ALL_PARTS
    relayed = shape((relay_rows, tok_rows), BF16)
    direct = shape((chunk_rows - relay_rows, tok_rows), BF16)
    chunk_flops = 2 * chunk_rows * tok_rows * features
    block = call(
        pack_kernel,
        (passing_rows, wk, wv, flat(anchor_keys), flat(anchor_values)),
        row(packed),
        4 * retained * tok_rows * size,
        in_specs=[HBM] * 5,
        scratch=[
            pltpu.VMEM(passing_rows.shape, jnp.int32),
            pltpu.VMEM((tok_rows, size), BF16),
            pltpu.VMEM((tok_rows, size), BF16),
            DMA((5,)),
        ],
    )
    query_rows = heads * tok_rows
    stats = (
        shape((1, query_rows), F32),
        shape((1, query_rows), F32),
        shape((size, query_rows), F32),
    )
    qh, hide, w_farther, w_far, *state = call(
        own_kernel,
        (block_of_device, queries.reshape(query_rows, size), wk, wv, out_weight),
        (row(query_rows), shape((slots, tok_rows), F32), weights(chunk_rows), weights(chunk_rows - relay_rows), *stats),
        4 * query_rows * tok_rows * size,
        in_specs=[HBM] * 5,
        scratch=[
            pltpu.SMEM((slots,), jnp.int32),
            pltpu.VMEM((query_rows, size), BF16),
            pltpu.VMEM((tok_rows, size), BF16),
            pltpu.VMEM((tok_rows, size), BF16),
            pltpu.VMEM((query_rows, size), F32),
            DMA((4 + 2 * PARTS,)),
        ],
    )
    order = [0]
    step = slots // 2
    held = block

    def exchange(mask):
        return lax.ppermute(held, "ctx", [(i, i ^ mask) for i in range(slots)])

    while step > 4:
        held = jnp.concatenate([held, exchange(step)], axis=0)
        order = order + [j ^ step for j in order]
        step //= 2
    diagonal, *sides = [exchange(mask) for mask in (6, 4, 2)]
    partner = exchange(1)
    across_chip = lambda order, mask: [j ^ mask for j in order]
    partner_order, diagonal_order = across_chip(order, 1), across_chip(order, 6)
    side_order = across_chip(order, 4) + across_chip(order, 2)
    blocks = lambda x: x.reshape(x.shape[0] // packed, packed, size)
    fold_flops = lambda n: 4 * query_rows * n * (anchors + retained) * size

    def attend(state, *pairs):
        orders, arrays = zip(*pairs)
        return call(
            functools.partial(early_kernel, orders, anchors, retained),
            (qh, hide, *[blocks(x) for x in arrays], *state),
            stats,
            fold_flops(sum(len(o) for o in orders)),
        )

    own_held, held = held, diagonal
    diagonal_partner = exchange(1)
    state = attend(state, (order, own_held), (partner_order, partner), (diagonal_order, diagonal))
    held = jnp.concatenate(sides, axis=0)
    other = exchange(1)
    state = attend(state, (across_chip(diagonal_order, 1), diagonal_partner), (side_order, held))
    late_order = across_chip(side_order, 1)
    att, first, far = call(
        functools.partial(late_kernel, (late_order,), anchors, retained),
        (qh, hide, blocks(other), *state, w_farther, w_far),
        (shape((features, tok_rows), BF16), relayed, direct),
        fold_flops(len(late_order)) + chunk_flops // 2,
    )

    def send(x, mask):
        return lax.ppermute(x, "tp", [(i, i ^ mask) for i in range(tp)])

    relay = send(first, 1)
    farther = call(direct_kernel, (att, w_farther), direct, chunk_flops)
    far = send(far, 2)
    farther = send(farther, 3)
    across, near_top, near_low = call(
        later_kernel,
        (att, out_weight),
        (relayed, relayed, direct),
        chunk_flops,
        in_specs=[VMEM, HBM],
        scratch=[pltpu.VMEM((relay_rows, features), BF16), pltpu.VMEM((chunk_rows, features), BF16), DMA((2 * PARTS,))],
    )
    near_low = send(near_low, 1)
    across = send(add(across, relay), 2)
    near_top = send(near_top, 1)
    own = call(
        own_chunk_kernel,
        (att, out_weight),
        chunk,
        chunk_flops,
        in_specs=[VMEM, HBM],
        scratch=[pltpu.VMEM((chunk_rows, features), BF16), DMA((PARTS,))],
    )
    top = add(own[:relay_rows], near_top, across)
    low = add(own[relay_rows:], near_low, far, farther)
    return jnp.concatenate([top, low], axis=0)


def solution(mesh):
    placed = (
        P("ctx", "tp", None),
        P("ctx", "tp", None),
        P("ctx", "tp", None),
        P("ctx", "tp", None),
        P("ctx", "tp", None),
        P(),
        P(),
        P(None, "tp"),
    )
    return jax.shard_map(layer, mesh=mesh, in_specs=placed, out_specs=P("tp", "ctx"), check_vma=False)
```

```python
import functools
import math

import jax
import jax.numpy as jnp
from jax import lax
from jax.experimental import pallas as pl
from jax.experimental.pallas import tpu as pltpu
from jax.sharding import PartitionSpec as P


BF16 = jnp.bfloat16
F32 = jnp.float32
HIDDEN = -1e30
VMEM = pl.BlockSpec(memory_space=pltpu.VMEM)
HBM = pl.BlockSpec(memory_space=pltpu.HBM)
DMA = pltpu.SemaphoreType.DMA
GROUP = 8
PARTS = 4
RELAY_PARTS, ALL_PARTS = 12, 16


def dot(a, b, a_dim, b_dim):
    return lax.dot_general(a, b, (((a_dim,), (b_dim,)), ((), ())), preferred_element_type=F32)


def call(kernel, inputs, out_shape, flops, in_specs=None, scratch=()):
    if in_specs:
        inputs = [pltpu.with_memory_space_constraint(x, pltpu.HBM) if s is HBM else x for x, s in zip(inputs, in_specs)]
    moved = sum(x.size * x.dtype.itemsize for x in inputs)
    return pl.pallas_call(
        kernel,
        out_shape=out_shape,
        in_specs=in_specs or [VMEM] * len(inputs),
        out_specs=jax.tree.map(lambda _: VMEM, out_shape),
        scratch_shapes=scratch,
        compiler_params=pltpu.CompilerParams(vmem_limit_bytes=32 << 20),
        cost_estimate=pl.CostEstimate(flops=flops, bytes_accessed=moved, transcendentals=0),
    )(*inputs)


def fetch(pairs, sems):
    copies = [pltpu.make_async_copy(a, b, sems.at[i]) for i, (a, b) in enumerate(pairs)]
    for copy in copies:
        copy.start()
    return copies


def wait(copies):
    for copy in copies:
        copy.wait()


def pack_kernel(rows_hbm, wk_hbm, wv_hbm, ak_hbm, av_hbm, out_ref, rows_ref, wk_ref, wv_ref, sems):
    anchors, retained = ak_hbm.shape[0], rows_ref.shape[1]
    first = 2 * anchors
    pairs = [
        (rows_hbm, rows_ref),
        (wk_hbm, wk_ref),
        (wv_hbm, wv_ref),
        (ak_hbm, out_ref.at[0:anchors, :]),
        (av_hbm, out_ref.at[anchors:first, :]),
    ]
    wait(fetch(pairs, sems))
    slot = lax.axis_index("ctx")
    chosen = rows_ref[pl.ds(slot, 1), :]
    places = lax.broadcasted_iota(jnp.int32, (wk_ref.shape[0], retained), 0)
    one_hot = (places == chosen).astype(BF16)
    out_ref[first : first + retained, :] = dot(one_hot, wk_ref[...], 0, 0).astype(BF16)
    out_ref[first + retained :, :] = dot(one_hot, wv_ref[...], 0, 0).astype(BF16)


def fold(q, before, groups, value_cols, factor):
    scores = jnp.concatenate([mask(dot(keys, q, 1, 1)) for keys, mask in groups], axis=0)
    top = jnp.max(scores, axis=0, keepdims=True)
    if before is not None:
        top = jnp.maximum(top, before[0])
    weights = jnp.exp2((scores - top) * factor)
    total = jnp.sum(weights, axis=0, keepdims=True)
    summed = dot(value_cols, weights.astype(BF16), 1, 0)
    if before is not None:
        fade = jnp.exp2((before[0] - top) * factor)
        total = total + before[1] * fade
        summed = summed + before[2] * fade
    return top, total, summed


def factor_of(size):
    return size ** (-0.5) * math.log2(math.e)


def parts_of(w_hbm, mask, first, w_ref):
    rows = w_ref.shape[0]
    begin = (lax.axis_index("tp") ^ mask) * (w_hbm.shape[0] // lax.axis_size("tp")) + first
    part = rows // PARTS
    return [
        (w_hbm.at[pl.ds(pl.multiple_of(begin + i, 16), part), :], w_ref.at[i : i + part, :])
        for i in range(0, rows, part)
    ]


def own_kernel(blocks_hbm, q_hbm, wk_hbm, wv_hbm, w_hbm,
               qh_ref, hide_ref, farther_ref, far_ref, top_ref, total_ref, summed_ref,
               blocks_ref, q_ref, wk_ref, wv_ref, qf_ref, sems):
    pairs = [(blocks_hbm, blocks_ref), (q_hbm, q_ref), (wk_hbm, wk_ref), (wv_hbm, wv_ref)]
    weights = parts_of(w_hbm, 3, 0, farther_ref)
    weights += parts_of(w_hbm, 2, farther_ref.shape[0] - far_ref.shape[0], far_ref)
    copies = fetch(pairs + weights, sems)
    wait(copies[: len(pairs)])
    tok_rows, size = wk_ref.shape
    heads = q_ref.shape[0] // tok_rows
    slot = lax.axis_index("ctx")
    own_block = blocks_ref[slot]
    for j in range(blocks_ref.shape[0]):
        bias = jnp.where(blocks_ref[slot ^ j] < own_block, 0.0, HIDDEN)
        hide_ref[j : j + 1, :] = jnp.full((1, hide_ref.shape[1]), bias, F32)
    qf_ref[...] = q_ref[...].astype(F32)
    lanes = GROUP * tok_rows
    key_at = lax.broadcasted_iota(jnp.int32, (tok_rows, lanes), 0)
    row_at = lax.broadcasted_iota(jnp.int32, (tok_rows, lanes), 1) % tok_rows
    causal = key_at <= row_at
    value_cols = wv_ref[...].T
    for h in range(0, heads, GROUP):
        for j in range(h, h + GROUP):
            qh_ref[j * tok_rows : (j + 1) * tok_rows, :] = qf_ref[
                pl.ds(j, tok_rows, stride=heads), :
            ].astype(BF16)
        cols = slice(h * tok_rows, (h + GROUP) * tok_rows)
        groups = [(wk_ref[...], lambda s: jnp.where(causal, s, HIDDEN))]
        state = fold(qh_ref[cols, :], None, groups, value_cols, factor_of(size))
        top_ref[:, cols], total_ref[:, cols], summed_ref[:, cols] = state
    wait(copies[len(pairs) :])


def rows_of(block_ref, anchors, retained):
    slots, _, size = block_ref.shape
    first = 2 * anchors
    take = lambda a, n: block_ref[:, a : a + n, :].reshape(slots * n, size)
    seen, past = take(0, anchors), take(first, retained)
    values = jnp.concatenate([take(anchors, anchors), take(first + retained, retained)], axis=0)
    return seen, past, values.T


def hidden_rows(hide_ref, order, retained, lanes):
    width = hide_ref.shape[1]
    rows = [jnp.broadcast_to(hide_ref[j : j + 1, :], (retained, width)) for j in order]
    column = jnp.concatenate(rows, axis=0)
    return jnp.concatenate([column] * (lanes // width), axis=1)


def fold_blocks(orders, anchors, retained, qh_ref, hide_ref, block_refs, state_refs, finish):
    top_ref, total_ref, summed_ref = state_refs
    tok_rows = hide_ref.shape[1]
    size = qh_ref.shape[1]
    heads = qh_ref.shape[0] // tok_rows
    groups, columns = [], []
    for order, block_ref in zip(orders, block_refs):
        seen, past, value_cols = rows_of(block_ref, anchors, retained)
        bias = hidden_rows(hide_ref, order, retained, GROUP * tok_rows)
        groups += [(seen, lambda s: s), (past, lambda s, bias=bias: s + bias)]
        columns.append(value_cols)
    value_cols = jnp.concatenate(columns, axis=1)
    for h in range(0, heads, GROUP):
        cols = slice(h * tok_rows, (h + GROUP) * tok_rows)
        before = (top_ref[:, cols], total_ref[:, cols], summed_ref[:, cols])
        finish(h, cols, fold(qh_ref[cols, :], before, groups, value_cols, factor_of(size)))


def early_kernel(orders, anchors, retained, qh_ref, hide_ref, *refs):
    block_refs, (top0, total0, summed0, top_ref, total_ref, summed_ref) = refs[: len(orders)], refs[len(orders) :]

    def finish(h, cols, state):
        top_ref[:, cols], total_ref[:, cols], summed_ref[:, cols] = state

    fold_blocks(orders, anchors, retained, qh_ref, hide_ref, block_refs, (top0, total0, summed0), finish)


def project(w_ref, first, att_ref, out_ref):
    rows = out_ref.shape[0]
    for start in range(0, rows, 256):
        stop = min(start + 256, rows)
        part = dot(w_ref[first + start : first + stop, :], att_ref[...], 1, 0)
        out_ref[start:stop, :] = part.astype(out_ref.dtype)


def late_kernel(orders, anchors, retained, qh_ref, hide_ref, block_ref, top0, total0, summed0, w_ref,
                att_ref, first_ref):
    tok_rows = hide_ref.shape[1]
    size = qh_ref.shape[1]

    def finish(h, cols, state):
        _, total, summed = state
        attended = (summed / total).astype(BF16)
        for j in range(GROUP):
            att_ref[(h + j) * size : (h + j + 1) * size, :] = attended[:, j * tok_rows : (j + 1) * tok_rows]

    fold_blocks(orders, anchors, retained, qh_ref, hide_ref, (block_ref,), (top0, total0, summed0), finish)
    project(w_ref, 0, att_ref, first_ref)


def direct_kernel(att_ref, farther_w, far_w, far_ref, farther_ref):
    project(far_w, 0, att_ref, far_ref)
    project(farther_w, farther_w.shape[0] - farther_ref.shape[0], att_ref, farther_ref)


def later_kernel(att_ref, w_hbm, across_ref, near_top_ref, near_low_ref, far_w, near_w, sems):
    copies = fetch(parts_of(w_hbm, 2, 0, far_w) + parts_of(w_hbm, 1, 0, near_w), sems)
    wait(copies)
    project(far_w, 0, att_ref, across_ref)
    project(near_w, 0, att_ref, near_top_ref)
    project(near_w, near_top_ref.shape[0], att_ref, near_low_ref)


def own_chunk_kernel(att_ref, w_hbm, out_ref, w_ref, sems):
    wait(fetch(parts_of(w_hbm, 0, 0, w_ref), sems))
    project(w_ref, 0, att_ref, out_ref)


def add(*parts):
    return functools.reduce(jnp.add, [p.astype(F32) for p in parts]).astype(BF16)


def layer(queries, window_keys, window_values, anchor_keys, anchor_values, passing_rows, block_of_device, out_weight):
    tok_rows, heads, size = queries.shape
    anchors, retained = anchor_keys.shape[0], passing_rows.shape[1]
    slots = block_of_device.shape[0]
    flat = lambda x: x.reshape(x.shape[0], size)
    wk, wv = flat(window_keys), flat(window_values)
    packed = 2 * (anchors + retained)
    shape = jax.ShapeDtypeStruct
    tp = lax.axis_size("tp")
    chunk_rows = out_weight.shape[0] // tp
    features = heads * size
    row = lambda n: shape((n, size), BF16)
    chunk = shape((chunk_rows, tok_rows), BF16)
    weights = lambda n: shape((n, features), BF16)
    relay_rows = chunk_rows * RELAY_PARTS // ALL_PARTS
    relayed = shape((relay_rows, tok_rows), BF16)
    direct = shape((chunk_rows - relay_rows, tok_rows), BF16)
    chunk_flops = 2 * chunk_rows * tok_rows * features
    block = call(
        pack_kernel,
        (passing_rows, wk, wv, flat(anchor_keys), flat(anchor_values)),
        row(packed),
        4 * retained * tok_rows * size,
        in_specs=[HBM] * 5,
        scratch=[
            pltpu.VMEM(passing_rows.shape, jnp.int32),
            pltpu.VMEM((tok_rows, size), BF16),
            pltpu.VMEM((tok_rows, size), BF16),
            DMA((5,)),
        ],
    )
    query_rows = heads * tok_rows
    stats = (
        shape((1, query_rows), F32),
        shape((1, query_rows), F32),
        shape((size, query_rows), F32),
    )
    qh, hide, w_farther, w_far, *state = call(
        own_kernel,
        (block_of_device, queries.reshape(query_rows, size), wk, wv, out_weight),
        (row(query_rows), shape((slots, tok_rows), F32), weights(chunk_rows), weights(chunk_rows - relay_rows), *stats),
        4 * query_rows * tok_rows * size,
        in_specs=[HBM] * 5,
        scratch=[
            pltpu.SMEM((slots,), jnp.int32),
            pltpu.VMEM((query_rows, size), BF16),
            pltpu.VMEM((tok_rows, size), BF16),
            pltpu.VMEM((tok_rows, size), BF16),
            pltpu.VMEM((query_rows, size), F32),
            DMA((4 + 2 * PARTS,)),
        ],
    )
    order = [0]
    step = slots // 2
    held = block

    def exchange(mask):
        return lax.ppermute(held, "ctx", [(i, i ^ mask) for i in range(slots)])

    while step > 4:
        held = jnp.concatenate([held, exchange(step)], axis=0)
        order = order + [j ^ step for j in order]
        step //= 2
    diagonal, *sides = [exchange(mask) for mask in (6, 4, 2)]
    partner = exchange(1)
    across_chip = lambda order, mask: [j ^ mask for j in order]
    partner_order, diagonal_order = across_chip(order, 1), across_chip(order, 6)
    side_order = across_chip(order, 4) + across_chip(order, 2)
    blocks = lambda x: x.reshape(x.shape[0] // packed, packed, size)
    fold_flops = lambda n: 4 * query_rows * n * (anchors + retained) * size

    def attend(state, *pairs):
        orders, arrays = zip(*pairs)
        return call(
            functools.partial(early_kernel, orders, anchors, retained),
            (qh, hide, *[blocks(x) for x in arrays], *state),
            stats,
            fold_flops(sum(len(o) for o in orders)),
        )

    own_held, held = held, diagonal
    diagonal_partner = exchange(1)
    state = attend(state, (order, own_held), (partner_order, partner), (diagonal_order, diagonal))
    held = jnp.concatenate(sides, axis=0)
    other = exchange(1)
    state = attend(state, (across_chip(diagonal_order, 1), diagonal_partner), (side_order, held))
    late_order = across_chip(side_order, 1)
    att, first = call(
        functools.partial(late_kernel, (late_order,), anchors, retained),
        (qh, hide, blocks(other), *state, w_farther),
        (shape((features, tok_rows), BF16), relayed),
        fold_flops(len(late_order)) + chunk_flops // 2,
    )

    def send(x, mask):
        return lax.ppermute(x, "tp", [(i, i ^ mask) for i in range(tp)])

    relay = send(first, 1)
    far, farther = call(direct_kernel, (att, w_farther, w_far), (direct, direct), chunk_flops)
    far = send(far, 2)
    farther = send(farther, 3)
    across, near_top, near_low = call(
        later_kernel,
        (att, out_weight),
        (relayed, relayed, direct),
        chunk_flops,
        in_specs=[VMEM, HBM],
        scratch=[pltpu.VMEM((relay_rows, features), BF16), pltpu.VMEM((chunk_rows, features), BF16), DMA((2 * PARTS,))],
    )
    near_low = send(near_low, 1)
    across = send(add(across, relay), 2)
    near_top = send(near_top, 1)
    own = call(
        own_chunk_kernel,
        (att, out_weight),
        chunk,
        chunk_flops,
        in_specs=[VMEM, HBM],
        scratch=[pltpu.VMEM((chunk_rows, features), BF16), DMA((PARTS,))],
    )
    top = add(own[:relay_rows], near_top, across)
    low = add(own[relay_rows:], near_low, far, farther)
    return jnp.concatenate([top, low], axis=0)


def solution(mesh):
    placed = (
        P("ctx", "tp", None),
        P("ctx", "tp", None),
        P("ctx", "tp", None),
        P("ctx", "tp", None),
        P("ctx", "tp", None),
        P(),
        P(),
        P(None, "tp"),
    )
    return jax.shard_map(layer, mesh=mesh, in_specs=placed, out_specs=P("tp", "ctx"), check_vma=False)
```

```python
import functools
import math

import jax
import jax.numpy as jnp
from jax import lax
from jax.experimental import pallas as pl
from jax.experimental.pallas import tpu as pltpu
from jax.sharding import PartitionSpec as P


BF16 = jnp.bfloat16
F32 = jnp.float32
HIDDEN = -1e30
VMEM = pl.BlockSpec(memory_space=pltpu.VMEM)
HBM = pl.BlockSpec(memory_space=pltpu.HBM)
DMA = pltpu.SemaphoreType.DMA
GROUP = 8
PARTS = 4
RELAY_PARTS, ALL_PARTS = 12, 16
NEAR_PARTS = 8


def dot(a, b, a_dim, b_dim):
    return lax.dot_general(a, b, (((a_dim,), (b_dim,)), ((), ())), preferred_element_type=F32)


def call(kernel, inputs, out_shape, flops, in_specs=None, scratch=()):
    if in_specs:
        inputs = [pltpu.with_memory_space_constraint(x, pltpu.HBM) if s is HBM else x for x, s in zip(inputs, in_specs)]
    moved = sum(x.size * x.dtype.itemsize for x in inputs)
    return pl.pallas_call(
        kernel,
        out_shape=out_shape,
        in_specs=in_specs or [VMEM] * len(inputs),
        out_specs=jax.tree.map(lambda _: VMEM, out_shape),
        scratch_shapes=scratch,
        compiler_params=pltpu.CompilerParams(vmem_limit_bytes=32 << 20),
        cost_estimate=pl.CostEstimate(flops=flops, bytes_accessed=moved, transcendentals=0),
    )(*inputs)


def fetch(pairs, sems):
    copies = [pltpu.make_async_copy(a, b, sems.at[i]) for i, (a, b) in enumerate(pairs)]
    for copy in copies:
        copy.start()
    return copies


def wait(copies):
    for copy in copies:
        copy.wait()


def pack_kernel(rows_hbm, wk_hbm, wv_hbm, ak_hbm, av_hbm, out_ref, rows_ref, wk_ref, wv_ref, sems):
    anchors, retained = ak_hbm.shape[0], rows_ref.shape[1]
    first = 2 * anchors
    pairs = [
        (rows_hbm, rows_ref),
        (wk_hbm, wk_ref),
        (wv_hbm, wv_ref),
        (ak_hbm, out_ref.at[0:anchors, :]),
        (av_hbm, out_ref.at[anchors:first, :]),
    ]
    wait(fetch(pairs, sems))
    slot = lax.axis_index("ctx")
    chosen = rows_ref[pl.ds(slot, 1), :]
    places = lax.broadcasted_iota(jnp.int32, (wk_ref.shape[0], retained), 0)
    one_hot = (places == chosen).astype(BF16)
    out_ref[first : first + retained, :] = dot(one_hot, wk_ref[...], 0, 0).astype(BF16)
    out_ref[first + retained :, :] = dot(one_hot, wv_ref[...], 0, 0).astype(BF16)


def fold(q, before, groups, value_cols, factor):
    scores = jnp.concatenate([mask(dot(keys, q, 1, 1)) for keys, mask in groups], axis=0)
    top = jnp.max(scores, axis=0, keepdims=True)
    if before is not None:
        top = jnp.maximum(top, before[0])
    weights = jnp.exp2((scores - top) * factor)
    total = jnp.sum(weights, axis=0, keepdims=True)
    summed = dot(value_cols, weights.astype(BF16), 1, 0)
    if before is not None:
        fade = jnp.exp2((before[0] - top) * factor)
        total = total + before[1] * fade
        summed = summed + before[2] * fade
    return top, total, summed


def factor_of(size):
    return size ** (-0.5) * math.log2(math.e)


def parts_of(w_hbm, mask, first, w_ref):
    rows = w_ref.shape[0]
    begin = (lax.axis_index("tp") ^ mask) * (w_hbm.shape[0] // lax.axis_size("tp")) + first
    part = rows // PARTS
    return [
        (w_hbm.at[pl.ds(pl.multiple_of(begin + i, 16), part), :], w_ref.at[i : i + part, :])
        for i in range(0, rows, part)
    ]


def own_kernel(blocks_hbm, q_hbm, wk_hbm, wv_hbm, w_hbm,
               qh_ref, hide_ref, farther_ref, far_ref, top_ref, total_ref, summed_ref,
               blocks_ref, q_ref, wk_ref, wv_ref, qf_ref, sems):
    pairs = [(blocks_hbm, blocks_ref), (q_hbm, q_ref), (wk_hbm, wk_ref), (wv_hbm, wv_ref)]
    weights = parts_of(w_hbm, 3, 0, farther_ref)
    weights += parts_of(w_hbm, 2, farther_ref.shape[0] - far_ref.shape[0], far_ref)
    copies = fetch(pairs + weights, sems)
    wait(copies[: len(pairs)])
    tok_rows, size = wk_ref.shape
    heads = q_ref.shape[0] // tok_rows
    slot = lax.axis_index("ctx")
    own_block = blocks_ref[slot]
    for j in range(blocks_ref.shape[0]):
        bias = jnp.where(blocks_ref[slot ^ j] < own_block, 0.0, HIDDEN)
        hide_ref[j : j + 1, :] = jnp.full((1, hide_ref.shape[1]), bias, F32)
    qf_ref[...] = q_ref[...].astype(F32)
    lanes = GROUP * tok_rows
    key_at = lax.broadcasted_iota(jnp.int32, (tok_rows, lanes), 0)
    row_at = lax.broadcasted_iota(jnp.int32, (tok_rows, lanes), 1) % tok_rows
    causal = key_at <= row_at
    value_cols = wv_ref[...].T
    for h in range(0, heads, GROUP):
        for j in range(h, h + GROUP):
            qh_ref[j * tok_rows : (j + 1) * tok_rows, :] = qf_ref[
                pl.ds(j, tok_rows, stride=heads), :
            ].astype(BF16)
        cols = slice(h * tok_rows, (h + GROUP) * tok_rows)
        groups = [(wk_ref[...], lambda s: jnp.where(causal, s, HIDDEN))]
        state = fold(qh_ref[cols, :], None, groups, value_cols, factor_of(size))
        top_ref[:, cols], total_ref[:, cols], summed_ref[:, cols] = state
    wait(copies[len(pairs) :])


def rows_of(block_ref, anchors, retained):
    slots, _, size = block_ref.shape
    first = 2 * anchors
    take = lambda a, n: block_ref[:, a : a + n, :].reshape(slots * n, size)
    seen, past = take(0, anchors), take(first, retained)
    values = jnp.concatenate([take(anchors, anchors), take(first + retained, retained)], axis=0)
    return seen, past, values.T


def hidden_rows(hide_ref, order, retained, lanes):
    width = hide_ref.shape[1]
    rows = [jnp.broadcast_to(hide_ref[j : j + 1, :], (retained, width)) for j in order]
    column = jnp.concatenate(rows, axis=0)
    return jnp.concatenate([column] * (lanes // width), axis=1)


def fold_blocks(orders, anchors, retained, qh_ref, hide_ref, block_refs, state_refs, finish):
    top_ref, total_ref, summed_ref = state_refs
    tok_rows = hide_ref.shape[1]
    size = qh_ref.shape[1]
    heads = qh_ref.shape[0] // tok_rows
    groups, columns = [], []
    for order, block_ref in zip(orders, block_refs):
        seen, past, value_cols = rows_of(block_ref, anchors, retained)
        bias = hidden_rows(hide_ref, order, retained, GROUP * tok_rows)
        groups += [(seen, lambda s: s), (past, lambda s, bias=bias: s + bias)]
        columns.append(value_cols)
    value_cols = jnp.concatenate(columns, axis=1)
    for h in range(0, heads, GROUP):
        cols = slice(h * tok_rows, (h + GROUP) * tok_rows)
        before = (top_ref[:, cols], total_ref[:, cols], summed_ref[:, cols])
        finish(h, cols, fold(qh_ref[cols, :], before, groups, value_cols, factor_of(size)))


def early_kernel(orders, anchors, retained, qh_ref, hide_ref, *refs):
    block_refs, (top0, total0, summed0, top_ref, total_ref, summed_ref) = refs[: len(orders)], refs[len(orders) :]

    def finish(h, cols, state):
        top_ref[:, cols], total_ref[:, cols], summed_ref[:, cols] = state

    fold_blocks(orders, anchors, retained, qh_ref, hide_ref, block_refs, (top0, total0, summed0), finish)


def project(w_ref, first, att_ref, out_ref):
    rows = out_ref.shape[0]
    for start in range(0, rows, 256):
        stop = min(start + 256, rows)
        part = dot(w_ref[first + start : first + stop, :], att_ref[...], 1, 0)
        out_ref[start:stop, :] = part.astype(out_ref.dtype)


def late_kernel(orders, anchors, retained, qh_ref, hide_ref, block_ref, top0, total0, summed0, w_ref,
                att_ref, first_ref):
    tok_rows = hide_ref.shape[1]
    size = qh_ref.shape[1]

    def finish(h, cols, state):
        _, total, summed = state
        attended = (summed / total).astype(BF16)
        for j in range(GROUP):
            att_ref[(h + j) * size : (h + j + 1) * size, :] = attended[:, j * tok_rows : (j + 1) * tok_rows]

    fold_blocks(orders, anchors, retained, qh_ref, hide_ref, (block_ref,), (top0, total0, summed0), finish)
    project(w_ref, 0, att_ref, first_ref)


def direct_kernel(att_ref, farther_w, far_w, far_ref, farther_ref):
    project(far_w, 0, att_ref, far_ref)
    project(farther_w, farther_w.shape[0] - farther_ref.shape[0], att_ref, farther_ref)


def later_kernel(att_ref, w_hbm, across_ref, near_top_ref, near_low_ref, far_w, near_w, sems):
    copies = fetch(parts_of(w_hbm, 2, 0, far_w) + parts_of(w_hbm, 1, 0, near_w), sems)
    wait(copies)
    project(far_w, 0, att_ref, across_ref)
    project(near_w, 0, att_ref, near_top_ref)
    project(near_w, near_top_ref.shape[0], att_ref, near_low_ref)


def own_chunk_kernel(att_ref, w_hbm, out_ref, w_ref, sems):
    wait(fetch(parts_of(w_hbm, 0, 0, w_ref), sems))
    project(w_ref, 0, att_ref, out_ref)


def add(*parts):
    return functools.reduce(jnp.add, [p.astype(F32) for p in parts]).astype(BF16)


def layer(queries, window_keys, window_values, anchor_keys, anchor_values, passing_rows, block_of_device, out_weight):
    tok_rows, heads, size = queries.shape
    anchors, retained = anchor_keys.shape[0], passing_rows.shape[1]
    slots = block_of_device.shape[0]
    flat = lambda x: x.reshape(x.shape[0], size)
    wk, wv = flat(window_keys), flat(window_values)
    packed = 2 * (anchors + retained)
    shape = jax.ShapeDtypeStruct
    tp = lax.axis_size("tp")
    chunk_rows = out_weight.shape[0] // tp
    features = heads * size
    row = lambda n: shape((n, size), BF16)
    chunk = shape((chunk_rows, tok_rows), BF16)
    weights = lambda n: shape((n, features), BF16)
    relay_rows = chunk_rows * RELAY_PARTS // ALL_PARTS
    relayed = shape((relay_rows, tok_rows), BF16)
    near_first = shape((chunk_rows * NEAR_PARTS // ALL_PARTS, tok_rows), BF16)
    near_rest = shape((chunk_rows - near_first.shape[0], tok_rows), BF16)
    direct = shape((chunk_rows - relay_rows, tok_rows), BF16)
    chunk_flops = 2 * chunk_rows * tok_rows * features
    block = call(
        pack_kernel,
        (passing_rows, wk, wv, flat(anchor_keys), flat(anchor_values)),
        row(packed),
        4 * retained * tok_rows * size,
        in_specs=[HBM] * 5,
        scratch=[
            pltpu.VMEM(passing_rows.shape, jnp.int32),
            pltpu.VMEM((tok_rows, size), BF16),
            pltpu.VMEM((tok_rows, size), BF16),
            DMA((5,)),
        ],
    )
    query_rows = heads * tok_rows
    stats = (
        shape((1, query_rows), F32),
        shape((1, query_rows), F32),
        shape((size, query_rows), F32),
    )
    qh, hide, w_farther, w_far, *state = call(
        own_kernel,
        (block_of_device, queries.reshape(query_rows, size), wk, wv, out_weight),
        (row(query_rows), shape((slots, tok_rows), F32), weights(chunk_rows), weights(chunk_rows - relay_rows), *stats),
        4 * query_rows * tok_rows * size,
        in_specs=[HBM] * 5,
        scratch=[
            pltpu.SMEM((slots,), jnp.int32),
            pltpu.VMEM((query_rows, size), BF16),
            pltpu.VMEM((tok_rows, size), BF16),
            pltpu.VMEM((tok_rows, size), BF16),
            pltpu.VMEM((query_rows, size), F32),
            DMA((4 + 2 * PARTS,)),
        ],
    )
    order = [0]
    step = slots // 2
    held = block

    def exchange(mask):
        return lax.ppermute(held, "ctx", [(i, i ^ mask) for i in range(slots)])

    while step > 4:
        held = jnp.concatenate([held, exchange(step)], axis=0)
        order = order + [j ^ step for j in order]
        step //= 2
    diagonal, *sides = [exchange(mask) for mask in (6, 4, 2)]
    partner = exchange(1)
    across_chip = lambda order, mask: [j ^ mask for j in order]
    partner_order, diagonal_order = across_chip(order, 1), across_chip(order, 6)
    side_order = across_chip(order, 4) + across_chip(order, 2)
    blocks = lambda x: x.reshape(x.shape[0] // packed, packed, size)
    fold_flops = lambda n: 4 * query_rows * n * (anchors + retained) * size

    def attend(state, *pairs):
        orders, arrays = zip(*pairs)
        return call(
            functools.partial(early_kernel, orders, anchors, retained),
            (qh, hide, *[blocks(x) for x in arrays], *state),
            stats,
            fold_flops(sum(len(o) for o in orders)),
        )

    own_held, held = held, diagonal
    diagonal_partner = exchange(1)
    state = attend(state, (order, own_held), (partner_order, partner), (diagonal_order, diagonal))
    held = jnp.concatenate(sides, axis=0)
    other = exchange(1)
    state = attend(state, (across_chip(diagonal_order, 1), diagonal_partner), (side_order, held))
    late_order = across_chip(side_order, 1)
    att, first = call(
        functools.partial(late_kernel, (late_order,), anchors, retained),
        (qh, hide, blocks(other), *state, w_farther),
        (shape((features, tok_rows), BF16), relayed),
        fold_flops(len(late_order)) + chunk_flops // 2,
    )

    def send(x, mask):
        return lax.ppermute(x, "tp", [(i, i ^ mask) for i in range(tp)])

    relay = send(first, 1)
    far, farther = call(direct_kernel, (att, w_farther, w_far), (direct, direct), chunk_flops)
    far = send(far, 2)
    farther = send(farther, 3)
    across, near_top, near_low = call(
        later_kernel,
        (att, out_weight),
        (relayed, near_first, near_rest),
        chunk_flops,
        in_specs=[VMEM, HBM],
        scratch=[pltpu.VMEM((relay_rows, features), BF16), pltpu.VMEM((chunk_rows, features), BF16), DMA((2 * PARTS,))],
    )
    near_low = send(near_low, 1)
    across = send(add(across, relay), 2)
    near_top = send(near_top, 1)
    own = call(
        own_chunk_kernel,
        (att, out_weight),
        chunk,
        chunk_flops,
        in_specs=[VMEM, HBM],
        scratch=[pltpu.VMEM((chunk_rows, features), BF16), DMA((PARTS,))],
    )
    near = jnp.concatenate([near_top, near_low], axis=0)
    top = add(own[:relay_rows], near[:relay_rows], across)
    low = add(own[relay_rows:], near[relay_rows:], far, farther)
    return jnp.concatenate([top, low], axis=0)


def solution(mesh):
    placed = (
        P("ctx", "tp", None),
        P("ctx", "tp", None),
        P("ctx", "tp", None),
        P("ctx", "tp", None),
        P("ctx", "tp", None),
        P(),
        P(),
        P(None, "tp"),
    )
    return jax.shard_map(layer, mesh=mesh, in_specs=placed, out_specs=P("tp", "ctx"), check_vma=False)
```
